512 devices in a mesh: dp: 32 (over y, x, core), expert: 16 (over z).
Axes of the slice: x: 4, y: 4, z: 16, core: 2. Of those that a mesh axis runs over, the one named last changes fastest.
Arguments:
- enc_out: bfloat16 [65536, 1408], P(('dp', 'expert')), may hold values from -40 to 40
- actions: int32 [65536], P(('dp', 'expert')), may hold values from 0 to 255
- enc_gain: float32 [1408], replicated, may hold values from 0.1 to 1.9
- enc_bias: float32 [1408], replicated, may hold values from -4 to 4
- embed_w: bfloat16 [1408, 1024], replicated, may hold values from -0.15625 to 0.15625
- action_table: bfloat16 [256, 1024], replicated, may hold values from -6 to 6
- pred_gain: float32 [1024], replicated, may hold values from 0.1 to 1.9
- router_w: bfloat16 [1024, 32], replicated, may hold values from -0.1875 to 0.1875
- up_w: bfloat16 [32, 1024, 768], P('expert', 'dp'), may hold values from -0.1875 to 0.1875
- down_w: bfloat16 [32, 768, 1024], P('expert', 'dp'), may hold values from -0.21875 to 0.21875
- cotangent: bfloat16 [65536, 1024], P(('dp', 'expert')), may hold values from -0.5 to 0.5
- routes: int32 [65536, 6], P(('dp', 'expert')), may hold values from 0 to 31, all different within a row; in each aligned block of 128 rows (0 to 127, 128 to 255, ...) at most 32 rows name the same one
Outputs:
- predicted: bfloat16 [65536, 1024], P(('dp', 'expert'))
- grad_down: bfloat16 [32, 768, 1024], P('expert', 'dp')
The draws below stay inside these ranges and needn't reach their ends.
Inputs may be any that keep to these rules, and one draw needn't show every extreme that they name: `routes`: within the 128 rows of one device each expert is named by at most 32 rows, a bound that some expert reaches in every such block.
All inputs are finite; a program needn't handle non-finite values.
Results may differ from the reference program's by a relative error of at most 0.017.
Values may be sent and summed in bfloat16 or wider, within the bound.
No kernel may reach another device: no remote copies, remote signals or barrier semaphores. Data moves between devices by JAX's collectives and lax.ppermute only.
A program may use at most 64 MiB of HBM per device.

```python
import math
import jax
import jax.numpy as jnp
import numpy as np
from jax import lax

ENC = 1408
D = 1024
HID = 768
EXPERTS = 32
TOPK = 6
ACTS = 256
TOK_DEV = 128
CAP = 32
TOKENS = 65536
N_DP = 32
N_EXPERT = 16


def draw_enc_out(key, part):
    keys = jax.random.split(jax.random.fold_in(key, 7), 3)
    row_scale = 10.0 ** jax.random.uniform(keys[1], (TOKENS, 1), jnp.float32, -0.5, 0.5)
    col_scale = 10.0 ** jax.random.uniform(keys[2], (1, ENC), jnp.float32, -0.5, 0.5)
    base = jax.random.normal(keys[0], (TOKENS, ENC), jnp.float32)
    base = jnp.clip(base, -4.0, 4.0)
    return (base * row_scale * col_scale).astype(jnp.bfloat16)


def with_ends(entries, own_key, smallest, largest):
    longest = entries.shape.index(max(entries.shape))
    spots = []
    for shift in (0, 1):
        where = [jax.random.randint(jax.random.fold_in(own_key, axis), (), 0, length) for axis, length in enumerate(entries.shape)]
        where[longest] = (where[longest] + shift) % entries.shape[longest]
        spots.append(tuple(where))
    return entries.at[spots[0]].set(smallest).at[spots[1]].set(largest)


def levels(rng, shape, cuts, least, largest):
    def one(position, parts):
        steps = jax.random.uniform(jax.random.fold_in(jax.random.fold_in(rng, 6), position), (parts,), jnp.float32, least / len(cuts), largest / len(cuts))
        return jnp.repeat(jnp.exp(steps), shape[position] // parts).reshape((-1,) + (1,) * (len(shape) - position - 1))

    loudness = one(*cuts[0])
    for cut in cuts[1:]:
        loudness = loudness * one(*cut)
    return loudness


def assign_block(stream_key, own, number, rows, amount, top, reach, lean):
    ranking = jax.random.permutation(stream_key, amount)
    crowded, common = shares(amount, rows * top, reach, lean, True), shares(amount, rows * top, reach, lean, False)
    places = jnp.arange(amount)

    def named(tallies, offset_by):
        used = int((tallies > 0).sum())
        fixed = max(1, used // 4)
        passed = fixed + (places - fixed + offset_by * (used - fixed)) % max(1, amount - fixed)
        return jnp.zeros((amount,), jnp.int32).at[ranking[jnp.where(places < fixed, places, passed)]].set(jnp.asarray(tallies, jnp.int32))

    tallies = jnp.where(number % 4 == 0, named(crowded, number // 4), named(common, number - number // 4 - 1))
    mixed = jax.random.permutation(jax.random.fold_in(own, 3), amount)
    donor, receiver = mixed[0:amount // 2 * 2:2], mixed[1:amount // 2 * 2:2]
    slack = jnp.minimum(tallies[donor] - 1, reach - tallies[receiver]) // 2
    slack = jnp.where((donor == ranking[0]) | (receiver == ranking[0]) | (tallies[receiver] == 0), 0, jnp.maximum(slack, 0))
    passed = jax.random.randint(jax.random.fold_in(own, 4), (amount // 2,), 0, 1 << 20) % (slack + 1)
    tallies = tallies.at[donor].add(-passed).at[receiver].add(passed)
    items = jnp.searchsorted(jnp.cumsum(tallies), jnp.arange(rows * top), side="right").astype(jnp.int32)
    table = items.reshape(top, rows).T
    table = table[jax.random.permutation(jax.random.fold_in(own, 1), rows)]
    offset_by = jax.random.randint(jax.random.fold_in(own, 2), (rows, 1), 0, top)
    return jnp.take_along_axis(table, (jnp.arange(top)[None, :] + offset_by) % top, axis=1)


def shares(amount, total, bound, lean, full):
    portions = [(1 << 20) // math.isqrt(grade ** lean) + 1 for grade in range(1, amount + 1)]
    largest = bound if full else min(bound, max(-(-total // amount), total * portions[0] // sum(portions)))
    least = 1 if total - largest >= amount - 1 else 0
    counts, spare = [largest] + [least] * (amount - 1), total - largest - least * (amount - 1)
    while spare > 0:
        free = [i for i in range(1, amount) if counts[i] < largest] or [i for i in range(1, amount) if counts[i] < bound]
        whole, budget = sum([portions[i] for i in free]), spare
        for i in free:
            more = min(bound - counts[i], max(1, budget * portions[i] // whole), spare)
            counts[i] = counts[i] + more
            spare = spare - more
    return np.array(counts)


def noise(stream_key, dims, deviation, bound, cuts=(), kind=jnp.bfloat16):
    entries = jax.random.normal(stream_key, dims, jnp.float32) * deviation
    if len(cuts) > 0:
        entries = levels(stream_key, dims, cuts, -0.22, 0.18) * entries
    return jnp.clip(entries, min=-bound, max=bound).astype(kind)


def setup_inputs(seed: int = 0) -> dict:
    splits = jax.random.split(jax.random.key(seed), 13)
    enc_out = draw_enc_out(jax.random.fold_in(splits[12], 71), 0)
    actions = with_ends(jax.random.randint(splits[1], (TOKENS,), 0, ACTS), jax.random.fold_in(splits[1], 1), 0, ACTS - 1).astype(jnp.int32)
    enc_gain = jnp.clip(1.0 + 0.18 * jax.random.normal(splits[2], (ENC,), jnp.float32), 0.1, 1.9)
    enc_bias = noise(splits[3], (ENC,), 1.0, 4.0, (), jnp.float32)
    embed_w = noise(splits[4], (ENC, D), ENC ** -0.5, 0.15625)
    action_table = noise(splits[5], (ACTS, D), 1.0, 6.0)
    pred_gain = jnp.clip(1.0 + 0.18 * jax.random.normal(splits[6], (D,), jnp.float32), 0.1, 1.9)
    router_w = noise(splits[7], (D, EXPERTS), D ** -0.5, 0.1875)
    up_w = noise(splits[8], (EXPERTS, D, HID), D ** -0.5, 0.1875, ((0, 16), (1, 32)))
    down_w = noise(splits[9], (EXPERTS, HID, D), HID ** -0.5, 0.21875, ((0, 16), (1, 32)))
    cotangent = noise(splits[10], (TOKENS, D), (4 * (TOKENS * TOPK // EXPERTS) ** -0.5), 0.5, ((0, 512),))
    routes_keys = jax.random.split(jax.random.fold_in(splits[11], 1), TOKENS // TOK_DEV)
    routes_turns = jax.random.permutation(jax.random.fold_in(splits[11], 3), TOKENS // TOK_DEV)
    routes = jax.vmap(lambda own, number: assign_block(jax.random.fold_in(splits[11], 2), own, number, TOK_DEV, EXPERTS, TOPK, CAP, 2))(routes_keys, routes_turns).reshape((TOKENS, TOPK))
    return dict(enc_out=enc_out, actions=actions, enc_gain=enc_gain, enc_bias=enc_bias, embed_w=embed_w, action_table=action_table, pred_gain=pred_gain, router_w=router_w, up_w=up_w, down_w=down_w, cotangent=cotangent, routes=routes)


def reference(enc_out, actions, enc_gain, enc_bias, embed_w, action_table, pred_gain, router_w, up_w, down_w, cotangent, routes):
    encoded = enc_out.astype(jnp.float32)
    center = encoded - lax.optimization_barrier(jnp.mean(encoded, axis=-1, keepdims=True))
    spread = lax.optimization_barrier(jnp.mean(center * center, axis=-1, keepdims=True))
    normed = (center * lax.rsqrt(spread + 1e-06) * enc_gain + enc_bias).astype(jnp.bfloat16)
    residual = jnp.dot(normed, embed_w, preferred_element_type=jnp.float32) + action_table[actions].astype(jnp.float32)
    scaled = (residual * lax.rsqrt(lax.optimization_barrier(jnp.mean(residual * residual, axis=-1, keepdims=True)) + 1e-06) * pred_gain).astype(jnp.bfloat16)
    logits = jnp.dot(scaled, router_w, preferred_element_type=jnp.float32)
    gate_values = jax.nn.sigmoid(jnp.take_along_axis(logits, routes, axis=1))
    block_count = N_DP * N_EXPERT
    pick_count = TOK_DEV * TOPK
    flat_routes = routes.reshape(block_count, pick_count)
    route_hits = (flat_routes[:, :, None] == jnp.arange(EXPERTS, dtype=jnp.int32)[None, None, :]).astype(jnp.int32)
    slot_rank = lax.optimization_barrier(jnp.sum((jnp.cumsum(route_hits, axis=1) - route_hits) * route_hits, axis=2)).astype(jnp.int32)
    row_tokens = N_EXPERT * TOK_DEV
    inputs = (scaled.reshape(N_DP, row_tokens, D), cotangent.reshape(N_DP, row_tokens, D), gate_values.reshape(N_DP, N_EXPERT, pick_count), flat_routes.reshape(N_DP, N_EXPERT, pick_count), slot_rank.reshape(N_DP, N_EXPERT, pick_count), residual.reshape(N_DP, row_tokens, D))
    up_float = up_w.astype(jnp.float32)
    down_float = down_w.astype(jnp.float32)

    def row_step(grad_total, row_items):
        row_scaled, row_cot, row_gates, row_routes, row_slots, row_resid = row_items
        source = jnp.broadcast_to(jnp.arange(N_EXPERT, dtype=jnp.int32)[:, None], row_routes.shape)
        token_rep = jnp.repeat(row_scaled, TOPK, axis=0).reshape(N_EXPERT, pick_count, D)
        cot_rep = jnp.repeat(row_cot, TOPK, axis=0).reshape(N_EXPERT, pick_count, D)
        gated_grad = (row_gates[:, :, None] * cot_rep.astype(jnp.float32)).astype(jnp.bfloat16)
        token_buf = jnp.zeros((EXPERTS, N_EXPERT, CAP, D), jnp.bfloat16).at[row_routes, source, row_slots].set(token_rep)
        grad_buf = jnp.zeros((EXPERTS, N_EXPERT, CAP, D), jnp.bfloat16).at[row_routes, source, row_slots].set(gated_grad)
        pre_act = jnp.einsum('escd,edh->esch', token_buf.astype(jnp.float32), up_float)
        hidden = jax.nn.gelu(pre_act, approximate=True).astype(jnp.bfloat16)
        hidden_float = hidden.astype(jnp.float32)
        expert_out = jnp.einsum('esch,ehd->escd', hidden_float, down_float).astype(jnp.bfloat16)
        partial_value = jnp.einsum('esch,escd->ehd', hidden_float, grad_buf.astype(jnp.float32)).astype(jnp.bfloat16)
        returned = expert_out[row_routes, source, row_slots].astype(jnp.float32)
        combined = lax.optimization_barrier(jnp.sum((row_gates[:, :, None] * returned).reshape(row_tokens, TOPK, D), axis=1))
        predicted = (row_resid + combined).astype(jnp.bfloat16)
        return (grad_total + partial_value.astype(jnp.float32), predicted)
    grad_total, predicted = lax.scan(row_step, jnp.zeros((EXPERTS, HID, D), jnp.float32), inputs)
    return (predicted.reshape(TOKENS, D), grad_total.astype(jnp.bfloat16))
```

```python
import jax
import jax.numpy as jnp
from jax import lax
from jax.sharding import PartitionSpec as P

EXPERTS = 32
TOPK = 6
CAP = 32


def exchange(rows):
    return lax.all_to_all(rows, "dp", split_axis=0, concat_axis=0, tiled=True)


def swap(pair):
    planes, chips = lax.axis_size("expert"), lax.axis_size("dp") // 2
    odd = lax.axis_index("dp") % 2 == 1
    same, other = jnp.where(odd, pair[1], pair[0]), jnp.where(odd, pair[0], pair[1])
    moved = []
    for flip, rows in ((0, same), (1, other)):
        perm = [
            ((2 * chip + core) * planes + z, (2 * z + (core ^ flip)) * planes + chip)
            for chip in range(chips)
            for core in range(2)
            for z in range(planes)
        ]
        moved.append(lax.ppermute(rows, ("dp", "expert"), perm))
    same, other = moved
    return jnp.stack([jnp.where(odd, other, same), jnp.where(odd, same, other)])


def per_device(
    enc_out,
    actions,
    enc_gain,
    enc_bias,
    embed_w,
    action_table,
    pred_gain,
    router_w,
    up_w,
    down_w,
    cotangent,
    routes,
):
    bf16, f32 = jnp.bfloat16, jnp.float32
    tokens, width = cotangent.shape
    hid_rows, up_cols = down_w.shape[1], up_w.shape[2]
    up_rows = up_w.shape[1]
    packed = jnp.concatenate(
        [jnp.pad(up_w, ((0, 0), (0, 0), (0, width - up_cols))), down_w], axis=1
    )
    weights = lax.all_gather(swap(packed), "expert", axis=0, tiled=True)
    up = weights[:, :up_rows, :up_cols].reshape(width, up_cols)
    down = weights[:, up_rows:, :].reshape(up_cols, width)

    experts = jnp.arange(EXPERTS, dtype=jnp.int32)
    hits = jnp.sum((routes.T[:, None, :] == experts[None, :, None]).astype(f32), axis=0)
    order = jnp.arange(tokens, dtype=jnp.int32)
    earlier = (order[:, None] < order[None, :]).astype(bf16)
    rank = jnp.dot(hits.astype(bf16), earlier, preferred_element_type=f32)
    place = jnp.where(hits > 0.0, rank.astype(jnp.int32), -1)
    slots = jnp.arange(CAP, dtype=jnp.int32)
    pick = (place[:, None, :] == slots[None, :, None]).reshape(EXPERTS * CAP, tokens)
    pick = pick.astype(bf16)

    got_cot = exchange(jnp.dot(pick, cotangent, preferred_element_type=f32).astype(bf16))

    encoded = enc_out.astype(f32)
    center = encoded - jnp.mean(encoded, axis=-1, keepdims=True)
    spread = jnp.mean(center * center, axis=-1, keepdims=True)
    normed = (center * lax.rsqrt(spread + 1e-06) * enc_gain + enc_bias).astype(bf16)
    onehot = (
        actions[:, None] == jnp.arange(action_table.shape[0], dtype=jnp.int32)[None, :]
    ).astype(bf16)
    residual = jnp.dot(normed, embed_w, preferred_element_type=f32) + jnp.dot(
        onehot, action_table, preferred_element_type=f32
    )
    scaled = (
        residual
        * lax.rsqrt(jnp.mean(residual * residual, axis=-1, keepdims=True) + 1e-06)
        * pred_gain
    ).astype(bf16)
    gates = jax.nn.sigmoid(
        lax.dot_general(
            router_w, scaled, (((0,), (1,)), ((), ())), preferred_element_type=f32
        )
    )
    got_tok = exchange(jnp.dot(pick, scaled, preferred_element_type=f32).astype(bf16))

    pre = jnp.dot(got_tok, up, preferred_element_type=f32)
    hidden = jax.nn.gelu(pre, approximate=True).astype(bf16)
    mine = experts == lax.axis_index("dp")
    all_gates = jax.nn.sigmoid(jnp.dot(got_tok, router_w, preferred_element_type=f32))
    gate = jnp.sum(jnp.where(mine[None, :], all_gates, 0.0), axis=1, keepdims=True)
    gated = (gate * got_cot.astype(f32)).astype(bf16)
    grad = lax.dot_general(
        hidden, gated, (((0,), (0,)), ((), ())), preferred_element_type=f32
    ).astype(bf16)
    summed = lax.psum_scatter(grad, "expert", scatter_dimension=0, tiled=True)
    grad_down = swap(summed.reshape(2, hid_rows, width))

    expert_out = jnp.dot(hidden, down, preferred_element_type=f32).astype(bf16)
    returned = exchange(expert_out)
    weight = pick.reshape(EXPERTS, CAP, tokens).astype(f32) * gates[:, None, :]
    weight = weight.reshape(EXPERTS * CAP, tokens)
    coarse = weight.astype(bf16)
    fine = (weight - coarse.astype(f32)).astype(bf16)
    dims = (((0,), (0,)), ((), ()))
    combined = lax.dot_general(
        coarse, returned, dims, preferred_element_type=f32
    ) + lax.dot_general(fine, returned, dims, preferred_element_type=f32)
    predicted = (residual + combined).astype(bf16)
    return (predicted, grad_down)


def solution(mesh):
    placed = (
        P(("dp", "expert"), None),
        P(("dp", "expert")),
        P(),
        P(),
        P(),
        P(),
        P(),
        P(),
        P("expert", "dp", None),
        P("expert", "dp", None),
        P(("dp", "expert"), None),
        P(("dp", "expert"), None),
    )
    return jax.shard_map(
        per_device,
        mesh=mesh,
        in_specs=placed,
        out_specs=(P(("dp", "expert"), None), P("expert", "dp", None)),
        check_vma=False,
    )
```

```python
import jax
import jax.numpy as jnp
from jax import lax
from jax.experimental import pallas as pl
from jax.experimental.pallas import tpu as pltpu
from jax.sharding import PartitionSpec as P

EXPERTS = 32
TOPK = 6
CAP = 32
PLANES = 16
CHIPS = 16
UP_ROWS = 32
PACK_ROWS = 48
STRIDE = 3
AXES = ("dp", "expert")


def home(plane, k):
    return plane ^ (10 * k)


def moves(flip, back):
    perm = []
    for chip in range(CHIPS):
        for core in range(2):
            for z in range(PLANES):
                k = core ^ flip
                here = (2 * chip + core) * PLANES + z
                there = (2 * home(z, k) + k) * PLANES + (chip + STRIDE * z) % PLANES
                perm.append((there, here) if back else (here, there))
    return perm


def swap(pair, odd, back):
    same, other = jnp.where(odd, pair[1], pair[0]), jnp.where(odd, pair[0], pair[1])
    return (
        lax.ppermute(same, AXES, moves(0, back)),
        lax.ppermute(other, AXES, moves(1, back)),
    )


def exchange(rows):
    return lax.all_to_all(rows, "dp", split_axis=0, concat_axis=0, tiled=True)


def hidden_kernel(info, w_ref, x_ref, cot_ref, router_ref, hid_ref, grad_ref, up_ref, gated_ref):
    first, odd, expert = info[0], info[1], info[2]
    f32, bf16 = jnp.float32, jnp.bfloat16
    cols = up_ref.shape[1]
    for block in range(2 * CHIPS):
        at = lax.rem(first + block // 2, PLANES)
        slot = (odd + block) & 1
        up_ref[block * UP_ROWS : (block + 1) * UP_ROWS, :] = w_ref[at, slot, :UP_ROWS, :cols]
    rows = x_ref.shape[0]
    step = 256
    for start in range(0, rows, step):
        part = pl.ds(start, step)
        x = x_ref[part, :]
        pre = jnp.dot(x, up_ref[...], preferred_element_type=f32)
        hid_ref[part, :] = jax.nn.gelu(pre, approximate=True).astype(bf16)
        gates = jax.nn.sigmoid(jnp.dot(x, router_ref[...], preferred_element_type=f32))
        mine = lax.broadcasted_iota(jnp.int32, gates.shape, 1) == expert
        gate = jnp.sum(jnp.where(mine, gates, 0.0), axis=1, keepdims=True)
        gated_ref[part, :] = (gate * cot_ref[part, :].astype(f32)).astype(bf16)
    group = grad_ref.shape[1]
    half = PLANES // 2
    for j in range(2):
        grad = lax.dot_general(
            hid_ref[:, j * half * group : (j + 1) * half * group],
            gated_ref[...],
            (((0,), (0,)), ((), ())),
            preferred_element_type=f32,
        ).astype(bf16)
        for i in range(half):
            at = lax.rem(first + j * half + i, PLANES)
            grad_ref[at] = grad[i * group : (i + 1) * group, :]


def out_kernel(info, w_ref, hid_ref, out_ref, wide_ref, down_ref):
    first, odd = info[0], info[1]
    cols = hid_ref.shape[1]
    width = out_ref.shape[1]
    spare = width - cols
    full = PACK_ROWS - UP_ROWS
    tail = UP_ROWS * spare // width
    for block in range(2 * CHIPS):
        at = lax.rem(first + block // 2, PLANES)
        slot = (odd + block) & 1
        base = block * (full + tail)
        wide_ref[base : base + full, :] = w_ref[at, slot, UP_ROWS:PACK_ROWS, :].astype(jnp.float32)
        rest = w_ref[at, slot, :UP_ROWS, cols:].astype(jnp.float32)
        for q in range(UP_ROWS // tail):
            wide_ref[base + full : base + full + tail, q * spare : (q + 1) * spare] = rest[
                q * tail : (q + 1) * tail, :
            ]
    down_ref[...] = wide_ref[...].astype(jnp.bfloat16)
    rows = hid_ref.shape[0]
    step = 256
    for start in range(0, rows, step):
        part = pl.ds(start, step)
        out_ref[part, :] = jnp.dot(
            hid_ref[part, :], down_ref[...], preferred_element_type=jnp.float32
        ).astype(jnp.bfloat16)


def per_device(
    enc_out,
    actions,
    enc_gain,
    enc_bias,
    embed_w,
    action_table,
    pred_gain,
    router_w,
    up_w,
    down_w,
    cotangent,
    routes,
):
    bf16, f32 = jnp.bfloat16, jnp.float32
    tokens, width = cotangent.shape
    up_cols = up_w.shape[2]
    hid_rows = down_w.shape[1]
    device = lax.axis_index("dp")
    chip, core = device // 2, device % 2
    odd = core == 1
    plane = jnp.where(odd, chip ^ 10, chip)
    info = jnp.stack([STRIDE * plane % PLANES, core, 2 * plane + core]).astype(jnp.int32)

    spare = width - up_cols
    full = PACK_ROWS - UP_ROWS
    rest = down_w[:, full:, :].reshape(2, hid_rows - full, width // spare, spare)
    rest = rest.transpose(0, 2, 1, 3).reshape(2, UP_ROWS, spare)
    packed = jnp.concatenate(
        [jnp.concatenate([up_w, rest], axis=2), down_w[:, :full, :]], axis=1
    )
    weights = lax.all_gather(
        jnp.stack(swap(packed, odd, False)), "expert", axis=0, tiled=True
    ).reshape(PLANES, 2, PACK_ROWS, width)

    names = [2 * home(d // 2, d % 2) + d % 2 for d in range(EXPERTS)]
    experts = jnp.array(names, dtype=jnp.int32)
    hits = jnp.sum((routes.T[:, None, :] == experts[None, :, None]).astype(f32), axis=0)
    order = jnp.arange(tokens, dtype=jnp.int32)
    earlier = (order[:, None] < order[None, :]).astype(bf16)
    rank = jnp.dot(hits.astype(bf16), earlier, preferred_element_type=f32)
    place = jnp.where(hits > 0.0, rank.astype(jnp.int32), -1)
    slots = jnp.arange(CAP, dtype=jnp.int32)
    pick = (place[:, None, :] == slots[None, :, None]).reshape(EXPERTS * CAP, tokens)
    pick = pick.astype(bf16)

    got_cot = exchange(jnp.dot(pick, cotangent, preferred_element_type=f32).astype(bf16))

    encoded = enc_out.astype(f32)
    center = encoded - jnp.mean(encoded, axis=-1, keepdims=True)
    spread = jnp.mean(center * center, axis=-1, keepdims=True)
    normed = (center * lax.rsqrt(spread + 1e-06) * enc_gain + enc_bias).astype(bf16)
    onehot = (
        actions[:, None] == jnp.arange(action_table.shape[0], dtype=jnp.int32)[None, :]
    ).astype(bf16)
    residual = jnp.dot(normed, embed_w, preferred_element_type=f32) + jnp.dot(
        onehot, action_table, preferred_element_type=f32
    )
    scaled = (
        residual
        * lax.rsqrt(jnp.mean(residual * residual, axis=-1, keepdims=True) + 1e-06)
        * pred_gain
    ).astype(bf16)
    got_tok = exchange(jnp.dot(pick, scaled, preferred_element_type=f32).astype(bf16))

    slots_all = EXPERTS * CAP
    smem = pl.BlockSpec(memory_space=pltpu.SMEM)
    vmem = pl.BlockSpec(memory_space=pltpu.VMEM)
    group = 2 * hid_rows
    hidden, grad = pl.pallas_call(
        hidden_kernel,
        out_shape=(
            jax.ShapeDtypeStruct((slots_all, up_cols), bf16),
            jax.ShapeDtypeStruct((PLANES, group, width), bf16),
        ),
        in_specs=[smem, vmem, vmem, vmem, vmem],
        out_specs=(vmem, vmem),
        scratch_shapes=[
            pltpu.VMEM((width, up_cols), bf16),
            pltpu.VMEM((slots_all, width), bf16),
        ],
        cost_estimate=pl.CostEstimate(
            flops=4 * slots_all * width * up_cols,
            bytes_accessed=11 << 20,
            transcendentals=slots_all * up_cols,
        ),
    )(info, weights, got_tok, got_cot, router_w)
    summed = lax.psum_scatter(grad, "expert", scatter_dimension=0, tiled=True)
    same, other = swap(summed.reshape(2, hid_rows, width), odd, True)
    grad_down = jnp.stack([jnp.where(odd, other, same), jnp.where(odd, same, other)])

    expert_out = pl.pallas_call(
        out_kernel,
        out_shape=jax.ShapeDtypeStruct((slots_all, width), bf16),
        in_specs=[smem, vmem, vmem],
        out_specs=vmem,
        scratch_shapes=[
            pltpu.VMEM((up_cols, width), f32),
            pltpu.VMEM((up_cols, width), bf16),
        ],
        cost_estimate=pl.CostEstimate(
            flops=2 * slots_all * width * up_cols,
            bytes_accessed=7 << 20,
            transcendentals=0,
        ),
    )(info, weights, hidden)
    returned = exchange(expert_out)
    logits = lax.dot_general(
        router_w, scaled, (((0,), (1,)), ((), ())), preferred_element_type=f32
    )
    gates = jnp.stack([logits[name] for name in names])
    gates = jax.nn.sigmoid(gates)
    weight = pick.reshape(EXPERTS, CAP, tokens).astype(f32) * gates[:, None, :]
    weight = weight.reshape(slots_all, tokens)
    coarse = weight.astype(bf16)
    fine = (weight - coarse.astype(f32)).astype(bf16)
    dims = (((0,), (0,)), ((), ()))
    combined = lax.dot_general(
        coarse, returned, dims, preferred_element_type=f32
    ) + lax.dot_general(fine, returned, dims, preferred_element_type=f32)
    predicted = (residual + combined).astype(bf16)
    return (predicted, grad_down)


def solution(mesh):
    placed = (
        P(("dp", "expert"), None),
        P(("dp", "expert")),
        P(),
        P(),
        P(),
        P(),
        P(),
        P(),
        P("expert", "dp", None),
        P("expert", "dp", None),
        P(("dp", "expert"), None),
        P(("dp", "expert"), None),
    )
    return jax.shard_map(
        per_device,
        mesh=mesh,
        in_specs=placed,
        out_specs=(P(("dp", "expert"), None), P("expert", "dp", None)),
        check_vma=False,
    )
```

```python
import jax
import jax.numpy as jnp
from jax import lax
from jax.experimental import pallas as pl
from jax.experimental.pallas import tpu as pltpu
from jax.sharding import PartitionSpec as P

EXPERTS = 32
TOPK = 6
CAP = 32
PLANES = 16
CHIPS = 16
RING = 8
UP_ROWS = 32
PACK_ROWS = 48
STRIDE = 5
AXES = ("dp", "expert")

NEAR, FAR = (0, 1, 7, 2, 6), (3, 5, 4)


def home(z, k):
    return z ^ (10 * k)


NAMES = [2 * home(m // 2, m % 2) + m % 2 for m in range(EXPERTS)]


def cells():
    groups = []
    for core in range(2):
        for pair in range(RING):
            z = (2 * pair, 2 * pair + 1) if core == 0 else (2 * pair + 2, 2 * pair + 1)
            groups.append(
                [(2 * chip + core) * PLANES + z[odd] % PLANES for chip in range(CHIPS) for odd in range(2)]
            )
    return groups


def moves(flip, back):
    perm = []
    for chip in range(CHIPS):
        for core in range(2):
            for z in range(PLANES):
                k = (chip & 1) ^ flip
                place = (chip // 2 + STRIDE * z) % RING
                here = (2 * chip + core) * PLANES + z
                there = (2 * home(z, k) + core) * PLANES + 2 * place + k
                perm.append((there, here) if back else (here, there))
    return perm


def upward(rows):
    return lax.ppermute(rows, "expert", [(z, (z + 2) % PLANES) for z in range(PLANES)])


def downward(rows):
    return lax.ppermute(rows, "expert", [(z, (z - 2) % PLANES) for z in range(PLANES)])


def across(rows):
    return lax.ppermute(rows, "dp", [(d, d ^ 1) for d in range(2 * CHIPS)])


def exchange(rows):
    return lax.all_to_all(
        rows, AXES, split_axis=0, concat_axis=0, tiled=True, axis_index_groups=cells()
    )


def dispatch_kernel(place_ref, tok_ref, cot_ref, out_ref):
    bf16 = jnp.bfloat16
    groups, tokens = place_ref.shape
    width = tok_ref.shape[1]
    step = 8
    slot = lax.broadcasted_iota(jnp.int32, (step, CAP, tokens), 1)
    for start in range(0, groups, step):
        place = place_ref[start : start + step, :]
        pick = (place[:, None, :] == slot).astype(jnp.float32).astype(bf16)
        pick = pick.reshape(step * CAP, tokens)
        for first, ref in ((0, tok_ref), (CAP, cot_ref)):
            rows = jnp.dot(pick, ref[...], preferred_element_type=jnp.float32).astype(bf16)
            out_ref[start : start + step, first : first + CAP, :] = rows.reshape(step, CAP, width)


def by_core(core, visit, own, other):
    @pl.when(core == 0)
    def _():
        visit(0, own)
        visit(1, other)

    @pl.when(core == 1)
    def _():
        visit(1, own)
        visit(0, other)


def hidden_kernel(
    info, own_near, own_far, other_near, other_far, got_ref, router_ref,
    hid_ref, keep_ref, give_ref, up_ref, gated_ref, grad_ref,
):
    first, k, core, expert = info[0], info[1], info[2], info[3]
    f32, bf16 = jnp.float32, jnp.bfloat16
    cols = up_ref.shape[2]
    width = got_ref.shape[2]

    def fill(parity, refs):
        for ref, away in zip(refs, (NEAR, FAR)):
            for i, r in enumerate(away):
                for slot in range(2):
                    at = 4 * ((first + r) & (RING - 1)) + 2 * ((k + slot) & 1) + parity
                    up_ref[at] = ref[i, slot, :UP_ROWS, :cols]

    by_core(core, fill, (own_near, own_far), (other_near, other_far))
    up = up_ref[...].reshape(width, cols)
    step = 8
    for start in range(0, EXPERTS, step):
        part = pl.ds(start * CAP, step * CAP)
        x = got_ref[start : start + step, :CAP, :].reshape(step * CAP, width)
        cot = got_ref[start : start + step, CAP:, :].reshape(step * CAP, width)
        pre = jnp.dot(x, up, preferred_element_type=f32)
        hid_ref[part, :] = jax.nn.gelu(pre, approximate=True).astype(bf16)
        gates = jax.nn.sigmoid(jnp.dot(x, router_ref[...], preferred_element_type=f32))
        mine = lax.broadcasted_iota(jnp.int32, gates.shape, 1) == expert
        gate = jnp.sum(jnp.where(mine, gates, 0.0), axis=1, keepdims=True)
        gated_ref[part, :] = (gate * cot.astype(f32)).astype(bf16)
    rows = keep_ref.shape[2]
    half = cols // 2
    for j in range(2):
        grad = lax.dot_general(
            hid_ref[:, j * half : (j + 1) * half],
            gated_ref[...],
            (((0,), (0,)), ((), ())),
            preferred_element_type=f32,
        )
        blocks = half // rows
        grad_ref[j * blocks : (j + 1) * blocks] = grad.reshape(blocks, rows, width)

    def store(parity, ref):
        for r in range(RING):
            for slot in range(2):
                at = 4 * ((first + r) & (RING - 1)) + 2 * ((k + slot) & 1) + parity
                ref[r, slot] = grad_ref[at].astype(bf16)

    by_core(core, store, keep_ref, give_ref)


def out_kernel(
    info, own_near, own_far, other_near, other_far, hid_ref, out_ref, wide_ref, down_ref
):
    first, k, core = info[0], info[1], info[2]
    f32, bf16 = jnp.float32, jnp.bfloat16
    cols, width = hid_ref.shape[1], out_ref.shape[1]
    spare = width - cols
    full = PACK_ROWS - UP_ROWS
    tail = UP_ROWS * spare // width

    def fill(parity, refs):
        for ref, away in zip(refs, (NEAR, FAR)):
            for i, r in enumerate(away):
                for slot in range(2):
                    at = 4 * ((first + r) & (RING - 1)) + 2 * ((k + slot) & 1) + parity
                    wide_ref[at, :full, :] = ref[i, slot, UP_ROWS:, :].astype(f32)
                    rest = ref[i, slot, :UP_ROWS, cols:].astype(f32)
                    for q in range(UP_ROWS // tail):
                        wide_ref[at, full:, q * spare : (q + 1) * spare] = rest[
                            q * tail : (q + 1) * tail, :
                        ]

    by_core(core, fill, (own_near, own_far), (other_near, other_far))
    down_ref[...] = wide_ref[...].reshape(cols, width).astype(bf16)
    rows = hid_ref.shape[0]
    step = 256
    for start in range(0, rows, step):
        part = pl.ds(start, step)
        out_ref[part, :] = jnp.dot(
            hid_ref[part, :], down_ref[...], preferred_element_type=f32
        ).astype(bf16)


def per_device(
    enc_out,
    actions,
    enc_gain,
    enc_bias,
    embed_w,
    action_table,
    pred_gain,
    router_w,
    up_w,
    down_w,
    cotangent,
    routes,
):
    bf16, f32 = jnp.bfloat16, jnp.float32
    tokens, width = cotangent.shape
    up_cols = up_w.shape[2]
    hid_rows = down_w.shape[1]
    device, z = lax.axis_index("dp"), lax.axis_index("expert")
    chip, core, k = device // 2, device % 2, z % 2
    odd = chip % 2 == 1
    origin = chip ^ (10 * k)
    first = (z // 2 - STRIDE * origin) % RING
    info = jnp.stack([first, k, core, 2 * origin + k]).astype(jnp.int32)

    spare = width - up_cols
    full = PACK_ROWS - UP_ROWS
    rest = down_w[:, full:, :].reshape(2, hid_rows - full, width // spare, spare)
    rest = rest.transpose(0, 2, 1, 3).reshape(2, UP_ROWS, spare)
    packed = jnp.concatenate(
        [jnp.concatenate([up_w, rest], axis=2), down_w[:, :full, :]], axis=1
    )
    same, other = jnp.where(odd, packed[1], packed[0]), jnp.where(odd, packed[0], packed[1])
    own = jnp.stack(
        [lax.ppermute(same, AXES, moves(0, False)), lax.ppermute(other, AXES, moves(1, False))]
    )

    experts = jnp.array(NAMES, dtype=jnp.int32)
    hits = jnp.sum((routes.T[:, None, :] == experts[None, :, None]).astype(f32), axis=0)
    order = jnp.arange(tokens, dtype=jnp.int32)
    earlier = (order[:, None] < order[None, :]).astype(bf16)
    rank = jnp.dot(hits.astype(bf16), earlier, preferred_element_type=f32)
    place = jnp.where(hits > 0.0, rank.astype(jnp.int32), -1)
    slots = jnp.arange(CAP, dtype=jnp.int32)
    pick = (place[:, None, :] == slots[None, :, None]).reshape(EXPERTS * CAP, tokens)
    pick = pick.astype(bf16)

    encoded = enc_out.astype(f32)
    center = encoded - jnp.mean(encoded, axis=-1, keepdims=True)
    spread = jnp.mean(center * center, axis=-1, keepdims=True)
    normed = (center * lax.rsqrt(spread + 1e-06) * enc_gain + enc_bias).astype(bf16)
    onehot = (
        actions[:, None] == jnp.arange(action_table.shape[0], dtype=jnp.int32)[None, :]
    ).astype(bf16)
    residual = jnp.dot(normed, embed_w, preferred_element_type=f32) + jnp.dot(
        onehot, action_table, preferred_element_type=f32
    )
    scaled = (
        residual
        * lax.rsqrt(jnp.mean(residual * residual, axis=-1, keepdims=True) + 1e-06)
        * pred_gain
    ).astype(bf16)
    smem = pl.BlockSpec(memory_space=pltpu.SMEM)
    vmem = pl.BlockSpec(memory_space=pltpu.VMEM)
    place, own = lax.optimization_barrier((place, own))
    sent = pl.pallas_call(
        dispatch_kernel,
        out_shape=jax.ShapeDtypeStruct((EXPERTS, 2 * CAP, width), bf16),
        in_specs=[vmem] * 3,
        out_specs=vmem,
        cost_estimate=pl.CostEstimate(
            flops=4 * EXPERTS * CAP * tokens * width, bytes_accessed=5 << 20, transcendentals=0
        ),
    )(place, scaled, cotangent)
    got = exchange(sent)

    below1, above1 = upward(own), downward(own)
    below2, above2 = upward(below1), downward(above1)
    own_near = jnp.stack([own, above1, below1, above2, below2])
    other_near = across(own_near)
    below3, above3 = upward(below2), downward(above2)
    opposite = jnp.stack([upward(below3[0]), downward(above3[1])])
    own_far = jnp.stack([above3, below3, opposite])
    other_far = across(own_far)
    weights = (own_near, own_far, other_near, other_far)

    slots_all = EXPERTS * CAP
    hidden, keep, give = pl.pallas_call(
        hidden_kernel,
        out_shape=(
            jax.ShapeDtypeStruct((slots_all, up_cols), bf16),
            jax.ShapeDtypeStruct((RING, 2, hid_rows, width), bf16),
            jax.ShapeDtypeStruct((RING, 2, hid_rows, width), bf16),
        ),
        in_specs=[smem] + [vmem] * 6,
        out_specs=(vmem, vmem, vmem),
        scratch_shapes=[
            pltpu.VMEM((EXPERTS, UP_ROWS, up_cols), bf16),
            pltpu.VMEM((slots_all, width), bf16),
            pltpu.VMEM((EXPERTS, hid_rows, width), f32),
        ],
        cost_estimate=pl.CostEstimate(
            flops=4 * slots_all * width * up_cols,
            bytes_accessed=11 << 20,
            transcendentals=slots_all * up_cols,
        ),
    )(info, *weights, got, router_w)
    gained = across(give)
    term = [keep[r].astype(f32) + gained[r].astype(f32) for r in range(RING)]
    rising = upward(term[4].astype(bf16))
    sinking = downward(term[5].astype(bf16))
    rising = upward((rising.astype(f32) + term[3]).astype(bf16))
    sinking = downward((sinking.astype(f32) + term[6]).astype(bf16))
    rising = upward((rising.astype(f32) + term[2]).astype(bf16))
    sinking = downward((sinking.astype(f32) + term[7]).astype(bf16))
    rising = upward((rising.astype(f32) + term[1]).astype(bf16))
    summed = (rising.astype(f32) + sinking.astype(f32) + term[0]).astype(bf16)
    same = lax.ppermute(summed[0], AXES, moves(0, True))
    other = lax.ppermute(summed[1], AXES, moves(1, True))
    grad_down = jnp.stack([jnp.where(odd, other, same), jnp.where(odd, same, other)])

    expert_out = pl.pallas_call(
        out_kernel,
        out_shape=jax.ShapeDtypeStruct((slots_all, width), bf16),
        in_specs=[smem] + [vmem] * 5,
        out_specs=vmem,
        scratch_shapes=[
            pltpu.VMEM((EXPERTS, hid_rows, width), f32),
            pltpu.VMEM((up_cols, width), bf16),
        ],
        cost_estimate=pl.CostEstimate(
            flops=2 * slots_all * width * up_cols,
            bytes_accessed=7 << 20,
            transcendentals=0,
        ),
    )(info, *weights, hidden)
    returned = exchange(expert_out.reshape(EXPERTS, CAP, width)).reshape(slots_all, width)
    logits = lax.dot_general(
        router_w, scaled, (((0,), (1,)), ((), ())), preferred_element_type=f32
    )
    gates = jnp.stack([logits[name] for name in NAMES])
    gates = jax.nn.sigmoid(gates)
    weight = pick.reshape(EXPERTS, CAP, tokens).astype(f32) * gates[:, None, :]
    weight = weight.reshape(slots_all, tokens)
    coarse = weight.astype(bf16)
    fine = (weight - coarse.astype(f32)).astype(bf16)
    dims = (((0,), (0,)), ((), ()))
    combined = lax.dot_general(
        coarse, returned, dims, preferred_element_type=f32
    ) + lax.dot_general(fine, returned, dims, preferred_element_type=f32)
    predicted = (residual + combined).astype(bf16)
    return (predicted, grad_down)


def solution(mesh):
    placed = (
        P(("dp", "expert"), None),
        P(("dp", "expert")),
        P(),
        P(),
        P(),
        P(),
        P(),
        P(),
        P("expert", "dp", None),
        P("expert", "dp", None),
        P(("dp", "expert"), None),
        P(("dp", "expert"), None),
    )
    return jax.shard_map(
        per_device,
        mesh=mesh,
        in_specs=placed,
        out_specs=(P(("dp", "expert"), None), P("expert", "dp", None)),
        check_vma=False,
    )
```

```python
import jax
import jax.numpy as jnp
from jax import lax
from jax.experimental import pallas as pl
from jax.experimental.pallas import tpu as pltpu
from jax.sharding import PartitionSpec as P

EXPERTS = 32
TOPK = 6
CAP = 32
PLANES = 16
CHIPS = 16
RING = 8
UP_ROWS = 32
PACK_ROWS = 48
STRIDE = 5
AXES = ("dp", "expert")


def home(z, k):
    return z ^ (10 * k)


NAMES = [2 * home(m // 2, m % 2) + m % 2 for m in range(EXPERTS)]


def cells():
    groups = []
    for core in range(2):
        for pair in range(RING):
            z = (2 * pair, 2 * pair + 1) if core == 0 else (2 * pair + 2, 2 * pair + 1)
            groups.append(
                [(2 * chip + core) * PLANES + z[odd] % PLANES for chip in range(CHIPS) for odd in range(2)]
            )
    return groups


def owners():
    return [
        [(2 * chip + core) * PLANES + z for z in range(k, PLANES, 2) for core in range(2)]
        for chip in range(CHIPS)
        for k in range(2)
    ]


def moves(back):
    perm = []
    for chip in range(CHIPS):
        for k in range(2):
            for z in range(PLANES):
                place = (chip // 2 + STRIDE * z) % RING
                here = (2 * chip + k) * PLANES + z
                there = (2 * home(z, k) + chip % 2) * PLANES + 2 * place + k
                perm.append((there, here) if back else (here, there))
    return perm


def across(rows):
    return lax.ppermute(rows, "dp", [(d, d ^ 1) for d in range(2 * CHIPS)])


def exchange(rows):
    return lax.all_to_all(
        rows, AXES, split_axis=0, concat_axis=0, tiled=True, axis_index_groups=cells()
    )


def dispatch_kernel(place_ref, tok_ref, cot_ref, out_ref):
    bf16 = jnp.bfloat16
    groups, tokens = place_ref.shape
    width = tok_ref.shape[1]
    step = 8
    slot = lax.broadcasted_iota(jnp.int32, (step, CAP, tokens), 1)
    for start in range(0, groups, step):
        place = place_ref[start : start + step, :]
        pick = (place[:, None, :] == slot).astype(jnp.float32).astype(bf16)
        pick = pick.reshape(step * CAP, tokens)
        for first, ref in ((0, tok_ref), (CAP, cot_ref)):
            rows = jnp.dot(pick, ref[...], preferred_element_type=jnp.float32).astype(bf16)
            out_ref[start : start + step, first : first + CAP, :] = rows.reshape(step, CAP, width)


def hidden_kernel(
    info, w_ref, got_ref, router_ref, hid_ref, keep_ref, give_ref, up_ref, gated_ref
):
    first, expert, core = info[0], info[1], info[2]
    f32, bf16 = jnp.float32, jnp.bfloat16
    cols = up_ref.shape[3]
    width = got_ref.shape[2]
    for chip in range(CHIPS):
        at = (first + chip // 2) & (RING - 1)
        for side in range(2):
            up_ref[chip, side] = w_ref[at, chip % 2, side, :UP_ROWS, :cols]
    up = up_ref[...].reshape(width, cols)
    step = 8
    for start in range(0, EXPERTS, step):
        part = pl.ds(start * CAP, step * CAP)
        x = got_ref[start : start + step, :CAP, :].reshape(step * CAP, width)
        cot = got_ref[start : start + step, CAP:, :].reshape(step * CAP, width)
        pre = jnp.dot(x, up, preferred_element_type=f32)
        hid_ref[part, :] = jax.nn.gelu(pre, approximate=True).astype(bf16)
        gates = jax.nn.sigmoid(jnp.dot(x, router_ref[...], preferred_element_type=f32))
        mine = lax.broadcasted_iota(jnp.int32, gates.shape, 1) == expert
        gate = jnp.sum(jnp.where(mine, gates, 0.0), axis=1, keepdims=True)
        gated_ref[part, :] = (gate * cot.astype(f32)).astype(bf16)
    rows = keep_ref.shape[1]
    half = CHIPS // 2
    for j in range(2):
        grad = lax.dot_general(
            hid_ref[:, j * half * rows : (j + 1) * half * rows],
            gated_ref[...],
            (((0,), (0,)), ((), ())),
            preferred_element_type=f32,
        ).astype(bf16)

        def store(parity, ref, j=j, grad=grad):
            for i in range(parity, half, 2):
                at = (first + (j * half + i) // 2) & (RING - 1)
                ref[at] = grad[i * rows : (i + 1) * rows, :]

        @pl.when(core == 0)
        def _(store=store):
            store(0, keep_ref)
            store(1, give_ref)

        @pl.when(core == 1)
        def _(store=store):
            store(1, keep_ref)
            store(0, give_ref)


def out_kernel(info, w_ref, hid_ref, out_ref, wide_ref, down_ref):
    first = info[0]
    f32, bf16 = jnp.float32, jnp.bfloat16
    cols, width = hid_ref.shape[1], out_ref.shape[1]
    spare = width - cols
    full = PACK_ROWS - UP_ROWS
    tail = UP_ROWS * spare // width
    for chip in range(CHIPS):
        at = (first + chip // 2) & (RING - 1)
        for core in range(2):
            wide_ref[chip, core, :full, :] = w_ref[at, chip % 2, core, UP_ROWS:, :].astype(f32)
            rest = w_ref[at, chip % 2, core, :UP_ROWS, cols:].astype(f32)
            for q in range(UP_ROWS // tail):
                wide_ref[chip, core, full:, q * spare : (q + 1) * spare] = rest[
                    q * tail : (q + 1) * tail, :
                ]
    down_ref[...] = wide_ref[...].reshape(cols, width).astype(bf16)
    rows = hid_ref.shape[0]
    step = 256
    for start in range(0, rows, step):
        part = pl.ds(start, step)
        out_ref[part, :] = jnp.dot(
            hid_ref[part, :], down_ref[...], preferred_element_type=f32
        ).astype(bf16)


def per_device(
    enc_out,
    actions,
    enc_gain,
    enc_bias,
    embed_w,
    action_table,
    pred_gain,
    router_w,
    up_w,
    down_w,
    cotangent,
    routes,
):
    bf16, f32 = jnp.bfloat16, jnp.float32
    tokens, width = cotangent.shape
    up_cols = up_w.shape[2]
    hid_rows = down_w.shape[1]
    device, z = lax.axis_index("dp"), lax.axis_index("expert")
    chip, core, k = device // 2, device % 2, z % 2
    odd = core == 1
    origin = chip ^ (10 * k)
    info = jnp.stack([STRIDE * origin % RING, 2 * origin + k, core]).astype(jnp.int32)

    spare = width - up_cols
    full = PACK_ROWS - UP_ROWS
    rest = down_w[:, full:, :].reshape(2, hid_rows - full, width // spare, spare)
    rest = rest.transpose(0, 2, 1, 3).reshape(2, UP_ROWS, spare)
    packed = jnp.concatenate(
        [jnp.concatenate([up_w, rest], axis=2), down_w[:, :full, :]], axis=1
    )
    mine = jnp.where(odd, packed[1], packed[0])
    theirs = across(jnp.where(odd, packed[0], packed[1]))
    theirs, enc_out, routes = lax.optimization_barrier((theirs, enc_out, routes))
    parts = jnp.stack([jnp.where(odd, theirs, mine), jnp.where(odd, mine, theirs)])
    own = lax.ppermute(parts, AXES, moves(False))
    experts = jnp.array(NAMES, dtype=jnp.int32)
    hits = jnp.sum((routes.T[:, None, :] == experts[None, :, None]).astype(f32), axis=0)
    order = jnp.arange(tokens, dtype=jnp.int32)
    earlier = (order[:, None] < order[None, :]).astype(bf16)
    rank = jnp.dot(hits.astype(bf16), earlier, preferred_element_type=f32)
    place = jnp.where(hits > 0.0, rank.astype(jnp.int32), -1)
    slots = jnp.arange(CAP, dtype=jnp.int32)
    pick = (place[:, None, :] == slots[None, :, None]).reshape(EXPERTS * CAP, tokens)
    pick = pick.astype(bf16)

    encoded = enc_out.astype(f32)
    center = encoded - jnp.mean(encoded, axis=-1, keepdims=True)
    spread = jnp.mean(center * center, axis=-1, keepdims=True)
    normed = (center * lax.rsqrt(spread + 1e-06) * enc_gain + enc_bias).astype(bf16)
    onehot = (
        actions[:, None] == jnp.arange(action_table.shape[0], dtype=jnp.int32)[None, :]
    ).astype(bf16)
    residual = jnp.dot(normed, embed_w, preferred_element_type=f32) + jnp.dot(
        onehot, action_table, preferred_element_type=f32
    )
    scaled = (
        residual
        * lax.rsqrt(jnp.mean(residual * residual, axis=-1, keepdims=True) + 1e-06)
        * pred_gain
    ).astype(bf16)
    own, place, scaled = lax.optimization_barrier((own, place, scaled))
    weights = lax.all_gather(
        own, AXES, axis=0, tiled=True, axis_index_groups=owners()
    ).reshape(RING, 2, 2, PACK_ROWS, width)
    smem = pl.BlockSpec(memory_space=pltpu.SMEM)
    vmem = pl.BlockSpec(memory_space=pltpu.VMEM)
    sent = pl.pallas_call(
        dispatch_kernel,
        out_shape=jax.ShapeDtypeStruct((EXPERTS, 2 * CAP, width), bf16),
        in_specs=[vmem] * 3,
        out_specs=vmem,
        cost_estimate=pl.CostEstimate(
            flops=4 * EXPERTS * CAP * tokens * width, bytes_accessed=5 << 20, transcendentals=0
        ),
    )(place, scaled, cotangent)
    got = exchange(sent)

    slots_all = EXPERTS * CAP
    hidden, keep, give = pl.pallas_call(
        hidden_kernel,
        out_shape=(
            jax.ShapeDtypeStruct((slots_all, up_cols), bf16),
            jax.ShapeDtypeStruct((RING, 2 * hid_rows, width), bf16),
            jax.ShapeDtypeStruct((RING, 2 * hid_rows, width), bf16),
        ),
        in_specs=[smem] + [vmem] * 3,
        out_specs=(vmem, vmem, vmem),
        scratch_shapes=[
            pltpu.VMEM((CHIPS, 2, UP_ROWS, up_cols), bf16),
            pltpu.VMEM((slots_all, width), bf16),
        ],
        cost_estimate=pl.CostEstimate(
            flops=4 * slots_all * width * up_cols,
            bytes_accessed=11 << 20,
            transcendentals=slots_all * up_cols,
        ),
    )(info, weights, got, router_w)
    pair = (keep.astype(f32) + across(give).astype(f32)).astype(bf16)
    parities = [list(range(k, PLANES, 2)) for k in range(2)]
    summed = lax.psum_scatter(
        pair, "expert", scatter_dimension=0, tiled=True, axis_index_groups=parities
    )
    both = lax.ppermute(summed.reshape(2, hid_rows, width), AXES, moves(True))
    kept = jnp.where(odd, both[1], both[0])
    given = across(jnp.where(odd, both[0], both[1]))
    grad_down = jnp.stack([jnp.where(odd, given, kept), jnp.where(odd, kept, given)])

    expert_out = pl.pallas_call(
        out_kernel,
        out_shape=jax.ShapeDtypeStruct((slots_all, width), bf16),
        in_specs=[smem] + [vmem] * 2,
        out_specs=vmem,
        scratch_shapes=[
            pltpu.VMEM((CHIPS, 2, hid_rows, width), f32),
            pltpu.VMEM((up_cols, width), bf16),
        ],
        cost_estimate=pl.CostEstimate(
            flops=2 * slots_all * width * up_cols,
            bytes_accessed=7 << 20,
            transcendentals=0,
        ),
    )(info, weights, hidden)
    returned = exchange(expert_out.reshape(EXPERTS, CAP, width)).reshape(slots_all, width)
    logits = lax.dot_general(
        router_w, scaled, (((0,), (1,)), ((), ())), preferred_element_type=f32
    )
    gates = jnp.stack([logits[name] for name in NAMES])
    gates = jax.nn.sigmoid(gates)
    weight = pick.reshape(EXPERTS, CAP, tokens).astype(f32) * gates[:, None, :]
    weight = weight.reshape(slots_all, tokens)
    coarse = weight.astype(bf16)
    fine = (weight - coarse.astype(f32)).astype(bf16)
    dims = (((0,), (0,)), ((), ()))
    combined = lax.dot_general(
        coarse, returned, dims, preferred_element_type=f32
    ) + lax.dot_general(fine, returned, dims, preferred_element_type=f32)
    predicted = (residual + combined).astype(bf16)
    return (predicted, grad_down)


def solution(mesh):
    placed = (
        P(("dp", "expert"), None),
        P(("dp", "expert")),
        P(),
        P(),
        P(),
        P(),
        P(),
        P(),
        P("expert", "dp", None),
        P("expert", "dp", None),
        P(("dp", "expert"), None),
        P(("dp", "expert"), None),
    )
    return jax.shard_map(
        per_device,
        mesh=mesh,
        in_specs=placed,
        out_specs=(P(("dp", "expert"), None), P("expert", "dp", None)),
        check_vma=False,
    )
```

```python
import jax
import jax.numpy as jnp
from jax import lax
from jax.experimental import pallas as pl
from jax.experimental.pallas import tpu as pltpu
from jax.sharding import PartitionSpec as P

EXPERTS = 32
TOPK = 6
CAP = 32
PLANES = 16
CHIPS = 16
UP_ROWS = 32
STRIDE = 3
AXES = ("dp", "expert")


def home(plane, k):
    return plane ^ (10 * k)


NAMES = [2 * home(m // 2, m % 2) + m % 2 for m in range(EXPERTS)]


def moves(flip, back):
    perm = []
    for chip in range(CHIPS):
        for core in range(2):
            for z in range(PLANES):
                k = core ^ flip
                here = (2 * chip + core) * PLANES + z
                there = (2 * home(z, k) + k) * PLANES + (chip + STRIDE * z) % PLANES
                perm.append((there, here) if back else (here, there))
    return perm


def swap(pair, odd, back):
    same, other = jnp.where(odd, pair[1], pair[0]), jnp.where(odd, pair[0], pair[1])
    return (
        lax.ppermute(same, AXES, moves(0, back)),
        lax.ppermute(other, AXES, moves(1, back)),
    )


def exchange(rows):
    return lax.all_to_all(rows, "dp", split_axis=0, concat_axis=0, tiled=True)


def dispatch_kernel(place_ref, tok_ref, cot_ref, out_ref):
    bf16 = jnp.bfloat16
    groups, tokens = place_ref.shape
    width = tok_ref.shape[1]
    step = 8
    slot = lax.broadcasted_iota(jnp.int32, (step, CAP, tokens), 1)
    for start in range(0, groups, step):
        place = place_ref[start : start + step, :]
        pick = (place[:, None, :] == slot).astype(jnp.float32).astype(bf16)
        pick = pick.reshape(step * CAP, tokens)
        for first, ref in ((0, tok_ref), (CAP, cot_ref)):
            rows = jnp.dot(pick, ref[...], preferred_element_type=jnp.float32).astype(bf16)
            out_ref[start : start + step, first : first + CAP, :] = rows.reshape(step, CAP, width)


def hidden_kernel(
    info, up0_ref, up1_ref, got_ref, router_ref, hid_ref, grad_ref, up_ref, gated_ref
):
    first, odd, expert = info[0], info[1], info[2]
    f32, bf16 = jnp.float32, jnp.bfloat16
    cols = up_ref.shape[3]
    width = got_ref.shape[2]
    for chip in range(CHIPS):
        at = lax.rem(first + chip, PLANES)
        for slot, ref in enumerate((up0_ref, up1_ref)):
            up_ref[chip, (odd + slot) & 1] = ref[at]
    up = up_ref[...].reshape(width, cols)
    step = 8
    for start in range(0, EXPERTS, step):
        part = pl.ds(start * CAP, step * CAP)
        x = got_ref[start : start + step, :CAP, :].reshape(step * CAP, width)
        cot = got_ref[start : start + step, CAP:, :].reshape(step * CAP, width)
        pre = jnp.dot(x, up, preferred_element_type=f32)
        hid_ref[part, :] = jax.nn.gelu(pre, approximate=True).astype(bf16)
        gates = jax.nn.sigmoid(jnp.dot(x, router_ref[...], preferred_element_type=f32))
        mine = lax.broadcasted_iota(jnp.int32, gates.shape, 1) == expert
        gate = jnp.sum(jnp.where(mine, gates, 0.0), axis=1, keepdims=True)
        gated_ref[part, :] = (gate * cot.astype(f32)).astype(bf16)
    rows = grad_ref.shape[1]
    half = CHIPS // 2
    for j in range(2):
        grad = lax.dot_general(
            hid_ref[:, j * half * rows : (j + 1) * half * rows],
            gated_ref[...],
            (((0,), (0,)), ((), ())),
            preferred_element_type=f32,
        ).astype(bf16)
        for i in range(half):
            at = lax.rem(first + j * half + i, PLANES)
            grad_ref[at] = grad[i * rows : (i + 1) * rows, :]


def out_kernel(info, w_ref, hid_ref, out_ref, wide_ref, down_ref):
    first, odd = info[0], info[1]
    f32, bf16 = jnp.float32, jnp.bfloat16
    cols, width = hid_ref.shape[1], out_ref.shape[1]
    for chip in range(CHIPS):
        at = lax.rem(first + chip, PLANES)
        for slot in range(2):
            wide_ref[chip, (odd + slot) & 1] = w_ref[at, slot].astype(f32)
    down_ref[...] = wide_ref[...].reshape(cols, width).astype(bf16)
    rows = hid_ref.shape[0]
    step = 256
    for start in range(0, rows, step):
        part = pl.ds(start, step)
        out_ref[part, :] = jnp.dot(
            hid_ref[part, :], down_ref[...], preferred_element_type=f32
        ).astype(bf16)


def per_device(
    enc_out,
    actions,
    enc_gain,
    enc_bias,
    embed_w,
    action_table,
    pred_gain,
    router_w,
    up_w,
    down_w,
    cotangent,
    routes,
):
    bf16, f32 = jnp.bfloat16, jnp.float32
    tokens, width = cotangent.shape
    up_cols = up_w.shape[2]
    hid_rows = down_w.shape[1]
    device = lax.axis_index("dp")
    chip, core = device // 2, device % 2
    odd = core == 1
    plane = jnp.where(odd, chip ^ 10, chip)
    info = jnp.stack([STRIDE * plane % PLANES, core, 2 * plane + core]).astype(jnp.int32)

    packed = jnp.concatenate(
        [jnp.pad(up_w, ((0, 0), (0, 0), (0, width - up_cols))), down_w], axis=1
    )
    own = swap(packed, odd, False)

    experts = jnp.array(NAMES, dtype=jnp.int32)
    hits = jnp.sum((routes.T[:, None, :] == experts[None, :, None]).astype(f32), axis=0)
    order = jnp.arange(tokens, dtype=jnp.int32)
    earlier = (order[:, None] < order[None, :]).astype(bf16)
    rank = jnp.dot(hits.astype(bf16), earlier, preferred_element_type=f32)
    place = jnp.where(hits > 0.0, rank.astype(jnp.int32), -1)
    slots = jnp.arange(CAP, dtype=jnp.int32)
    pick = (place[:, None, :] == slots[None, :, None]).reshape(EXPERTS * CAP, tokens)
    pick = pick.astype(bf16)

    encoded = enc_out.astype(f32)
    center = encoded - jnp.mean(encoded, axis=-1, keepdims=True)
    spread = jnp.mean(center * center, axis=-1, keepdims=True)
    normed = (center * lax.rsqrt(spread + 1e-06) * enc_gain + enc_bias).astype(bf16)
    onehot = (
        actions[:, None] == jnp.arange(action_table.shape[0], dtype=jnp.int32)[None, :]
    ).astype(bf16)
    residual = jnp.dot(normed, embed_w, preferred_element_type=f32) + jnp.dot(
        onehot, action_table, preferred_element_type=f32
    )
    scaled = (
        residual
        * lax.rsqrt(jnp.mean(residual * residual, axis=-1, keepdims=True) + 1e-06)
        * pred_gain
    ).astype(bf16)
    smem = pl.BlockSpec(memory_space=pltpu.SMEM)
    vmem = pl.BlockSpec(memory_space=pltpu.VMEM)
    own, place, scaled = lax.optimization_barrier((own, place, scaled))
    sent = pl.pallas_call(
        dispatch_kernel,
        out_shape=jax.ShapeDtypeStruct((EXPERTS, 2 * CAP, width), bf16),
        in_specs=[vmem] * 3,
        out_specs=vmem,
        cost_estimate=pl.CostEstimate(
            flops=4 * EXPERTS * CAP * tokens * width, bytes_accessed=5 << 20, transcendentals=0
        ),
    )(place, scaled, cotangent)
    got = exchange(sent)
    down = lax.all_gather(
        jnp.stack([part[UP_ROWS:] for part in own]), "expert", axis=0, tiled=True
    ).reshape(PLANES, 2, hid_rows, width)
    ups, sent = lax.optimization_barrier(([part[:UP_ROWS, :up_cols] for part in own], sent))
    ups = [lax.all_gather(part, "expert", axis=0) for part in ups]

    slots_all = EXPERTS * CAP
    hidden, grad = pl.pallas_call(
        hidden_kernel,
        out_shape=(
            jax.ShapeDtypeStruct((slots_all, up_cols), bf16),
            jax.ShapeDtypeStruct((PLANES, 2 * hid_rows, width), bf16),
        ),
        in_specs=[smem] + [vmem] * 4,
        out_specs=(vmem, vmem),
        scratch_shapes=[
            pltpu.VMEM((CHIPS, 2, UP_ROWS, up_cols), bf16),
            pltpu.VMEM((slots_all, width), bf16),
        ],
        cost_estimate=pl.CostEstimate(
            flops=4 * slots_all * width * up_cols,
            bytes_accessed=11 << 20,
            transcendentals=slots_all * up_cols,
        ),
    )(info, *ups, got, router_w)
    summed = lax.psum_scatter(grad, "expert", scatter_dimension=0, tiled=True)
    same, other = swap(summed.reshape(2, hid_rows, width), odd, True)
    grad_down = jnp.stack([jnp.where(odd, other, same), jnp.where(odd, same, other)])

    expert_out = pl.pallas_call(
        out_kernel,
        out_shape=jax.ShapeDtypeStruct((slots_all, width), bf16),
        in_specs=[smem] + [vmem] * 2,
        out_specs=vmem,
        scratch_shapes=[
            pltpu.VMEM((CHIPS, 2, hid_rows, width), f32),
            pltpu.VMEM((up_cols, width), bf16),
        ],
        cost_estimate=pl.CostEstimate(
            flops=2 * slots_all * width * up_cols,
            bytes_accessed=7 << 20,
            transcendentals=0,
        ),
    )(info, down, hidden)
    returned = exchange(expert_out.reshape(EXPERTS, CAP, width)).reshape(slots_all, width)
    logits = lax.dot_general(
        router_w, scaled, (((0,), (1,)), ((), ())), preferred_element_type=f32
    )
    gates = jnp.stack([logits[name] for name in NAMES])
    gates = jax.nn.sigmoid(gates)
    weight = pick.reshape(EXPERTS, CAP, tokens).astype(f32) * gates[:, None, :]
    weight = weight.reshape(slots_all, tokens)
    coarse = weight.astype(bf16)
    fine = (weight - coarse.astype(f32)).astype(bf16)
    dims = (((0,), (0,)), ((), ()))
    combined = lax.dot_general(
        coarse, returned, dims, preferred_element_type=f32
    ) + lax.dot_general(fine, returned, dims, preferred_element_type=f32)
    predicted = (residual + combined).astype(bf16)
    return (predicted, grad_down)


def solution(mesh):
    placed = (
        P(("dp", "expert"), None),
        P(("dp", "expert")),
        P(),
        P(),
        P(),
        P(),
        P(),
        P(),
        P("expert", "dp", None),
        P("expert", "dp", None),
        P(("dp", "expert"), None),
        P(("dp", "expert"), None),
    )
    return jax.shard_map(
        per_device,
        mesh=mesh,
        in_specs=placed,
        out_specs=(P(("dp", "expert"), None), P("expert", "dp", None)),
        check_vma=False,
    )
```

```python
import jax
import jax.numpy as jnp
from jax import lax
from jax.experimental import pallas as pl
from jax.experimental.pallas import tpu as pltpu
from jax.sharding import PartitionSpec as P

EXPERTS = 32
TOPK = 6
CAP = 32
PLANES = 16
CHIPS = 16
UP_ROWS = 32
PACK_ROWS = 48
STRIDE = 3
AXES = ("dp", "expert")


def home(plane, k):
    return plane ^ (10 * k)


NAMES = [2 * home(m // 2, m % 2) + m % 2 for m in range(EXPERTS)]


def moves(flip, back):
    perm = []
    for chip in range(CHIPS):
        for core in range(2):
            for z in range(PLANES):
                k = core ^ flip
                here = (2 * chip + core) * PLANES + z
                there = (2 * home(z, k) + k) * PLANES + (chip + STRIDE * z) % PLANES
                perm.append((there, here) if back else (here, there))
    return perm


def swap(pair, odd, back):
    same, other = jnp.where(odd, pair[1], pair[0]), jnp.where(odd, pair[0], pair[1])
    return (
        lax.ppermute(same, AXES, moves(0, back)),
        lax.ppermute(other, AXES, moves(1, back)),
    )


def exchange(rows):
    return lax.all_to_all(rows, "dp", split_axis=0, concat_axis=0, tiled=True)


def dispatch_kernel(place_ref, tok_ref, cot_ref, out_ref):
    bf16 = jnp.bfloat16
    groups, tokens = place_ref.shape
    width = tok_ref.shape[1]
    step = 8
    slot = lax.broadcasted_iota(jnp.int32, (step, CAP, tokens), 1)
    for start in range(0, groups, step):
        place = place_ref[start : start + step, :]
        pick = (place[:, None, :] == slot).astype(jnp.float32).astype(bf16)
        pick = pick.reshape(step * CAP, tokens)
        for first, ref in ((0, tok_ref), (CAP, cot_ref)):
            rows = jnp.dot(pick, ref[...], preferred_element_type=jnp.float32).astype(bf16)
            out_ref[start : start + step, first : first + CAP, :] = rows.reshape(step, CAP, width)


def hidden_kernel(
    info, w_ref, got_ref, router_ref, hid_ref, grad_ref, up_ref, gated_ref
):
    first, odd, expert = info[0], info[1], info[2]
    f32, bf16 = jnp.float32, jnp.bfloat16
    cols = up_ref.shape[3]
    width = got_ref.shape[2]
    for chip in range(CHIPS):
        at = lax.rem(first + chip, PLANES)
        for slot in range(2):
            up_ref[chip, (odd + slot) & 1] = w_ref[at, slot, :UP_ROWS, :cols]
    up = up_ref[...].reshape(width, cols)
    step = 8
    for start in range(0, EXPERTS, step):
        part = pl.ds(start * CAP, step * CAP)
        x = got_ref[start : start + step, :CAP, :].reshape(step * CAP, width)
        cot = got_ref[start : start + step, CAP:, :].reshape(step * CAP, width)
        pre = jnp.dot(x, up, preferred_element_type=f32)
        hid_ref[part, :] = jax.nn.gelu(pre, approximate=True).astype(bf16)
        gates = jax.nn.sigmoid(jnp.dot(x, router_ref[...], preferred_element_type=f32))
        mine = lax.broadcasted_iota(jnp.int32, gates.shape, 1) == expert
        gate = jnp.sum(jnp.where(mine, gates, 0.0), axis=1, keepdims=True)
        gated_ref[part, :] = (gate * cot.astype(f32)).astype(bf16)
    rows = grad_ref.shape[1]
    half = CHIPS // 2
    for j in range(2):
        grad = lax.dot_general(
            hid_ref[:, j * half * rows : (j + 1) * half * rows],
            gated_ref[...],
            (((0,), (0,)), ((), ())),
            preferred_element_type=f32,
        ).astype(bf16)
        for i in range(half):
            at = lax.rem(first + j * half + i, PLANES)
            grad_ref[at] = grad[i * rows : (i + 1) * rows, :]


def out_kernel(info, w_ref, hid_ref, out_ref, wide_ref, down_ref):
    first, odd = info[0], info[1]
    f32, bf16 = jnp.float32, jnp.bfloat16
    cols, width = hid_ref.shape[1], out_ref.shape[1]
    spare = width - cols
    full = PACK_ROWS - UP_ROWS
    tail = UP_ROWS * spare // width
    for chip in range(CHIPS):
        at = lax.rem(first + chip, PLANES)
        for slot in range(2):
            side = (odd + slot) & 1
            wide_ref[chip, side, :full, :] = w_ref[at, slot, UP_ROWS:, :].astype(f32)
            rest = w_ref[at, slot, :UP_ROWS, cols:].astype(f32)
            for q in range(UP_ROWS // tail):
                wide_ref[chip, side, full:, q * spare : (q + 1) * spare] = rest[
                    q * tail : (q + 1) * tail, :
                ]
    down_ref[...] = wide_ref[...].reshape(cols, width).astype(bf16)
    rows = hid_ref.shape[0]
    step = 256
    for start in range(0, rows, step):
        part = pl.ds(start, step)
        out_ref[part, :] = jnp.dot(
            hid_ref[part, :], down_ref[...], preferred_element_type=f32
        ).astype(bf16)


def per_device(
    enc_out,
    actions,
    enc_gain,
    enc_bias,
    embed_w,
    action_table,
    pred_gain,
    router_w,
    up_w,
    down_w,
    cotangent,
    routes,
):
    bf16, f32 = jnp.bfloat16, jnp.float32
    tokens, width = cotangent.shape
    up_cols = up_w.shape[2]
    hid_rows = down_w.shape[1]
    device = lax.axis_index("dp")
    chip, core = device // 2, device % 2
    odd = core == 1
    plane = jnp.where(odd, chip ^ 10, chip)
    info = jnp.stack([STRIDE * plane % PLANES, core, 2 * plane + core]).astype(jnp.int32)

    spare = width - up_cols
    full = PACK_ROWS - UP_ROWS
    rest = down_w[:, full:, :].reshape(2, hid_rows - full, width // spare, spare)
    rest = rest.transpose(0, 2, 1, 3).reshape(2, UP_ROWS, spare)
    packed = jnp.concatenate(
        [jnp.concatenate([up_w, rest], axis=2), down_w[:, :full, :]], axis=1
    )
    own = swap(packed, odd, False)

    experts = jnp.array(NAMES, dtype=jnp.int32)
    hits = jnp.sum((routes.T[:, None, :] == experts[None, :, None]).astype(f32), axis=0)
    order = jnp.arange(tokens, dtype=jnp.int32)
    earlier = (order[:, None] < order[None, :]).astype(bf16)
    rank = jnp.dot(hits.astype(bf16), earlier, preferred_element_type=f32)
    place = jnp.where(hits > 0.0, rank.astype(jnp.int32), -1)
    slots = jnp.arange(CAP, dtype=jnp.int32)
    pick = (place[:, None, :] == slots[None, :, None]).reshape(EXPERTS * CAP, tokens)
    pick = pick.astype(bf16)

    encoded = enc_out.astype(f32)
    center = encoded - jnp.mean(encoded, axis=-1, keepdims=True)
    spread = jnp.mean(center * center, axis=-1, keepdims=True)
    normed = (center * lax.rsqrt(spread + 1e-06) * enc_gain + enc_bias).astype(bf16)
    onehot = (
        actions[:, None] == jnp.arange(action_table.shape[0], dtype=jnp.int32)[None, :]
    ).astype(bf16)
    residual = jnp.dot(normed, embed_w, preferred_element_type=f32) + jnp.dot(
        onehot, action_table, preferred_element_type=f32
    )
    scaled = (
        residual
        * lax.rsqrt(jnp.mean(residual * residual, axis=-1, keepdims=True) + 1e-06)
        * pred_gain
    ).astype(bf16)
    smem = pl.BlockSpec(memory_space=pltpu.SMEM)
    vmem = pl.BlockSpec(memory_space=pltpu.VMEM)
    own, place, scaled = lax.optimization_barrier((own, place, scaled))
    sent = pl.pallas_call(
        dispatch_kernel,
        out_shape=jax.ShapeDtypeStruct((EXPERTS, 2 * CAP, width), bf16),
        in_specs=[vmem] * 3,
        out_specs=vmem,
        cost_estimate=pl.CostEstimate(
            flops=4 * EXPERTS * CAP * tokens * width, bytes_accessed=5 << 20, transcendentals=0
        ),
    )(place, scaled, cotangent)
    got = exchange(sent)
    weights = lax.all_gather(jnp.stack(own), "expert", axis=0, tiled=True)
    weights = weights.reshape(PLANES, 2, PACK_ROWS, width)

    slots_all = EXPERTS * CAP
    hidden, grad = pl.pallas_call(
        hidden_kernel,
        out_shape=(
            jax.ShapeDtypeStruct((slots_all, up_cols), bf16),
            jax.ShapeDtypeStruct((PLANES, 2 * hid_rows, width), bf16),
        ),
        in_specs=[smem] + [vmem] * 3,
        out_specs=(vmem, vmem),
        scratch_shapes=[
            pltpu.VMEM((CHIPS, 2, UP_ROWS, up_cols), bf16),
            pltpu.VMEM((slots_all, width), bf16),
        ],
        cost_estimate=pl.CostEstimate(
            flops=4 * slots_all * width * up_cols,
            bytes_accessed=11 << 20,
            transcendentals=slots_all * up_cols,
        ),
    )(info, weights, got, router_w)
    summed = lax.psum_scatter(grad, "expert", scatter_dimension=0, tiled=True)
    same, other = swap(summed.reshape(2, hid_rows, width), odd, True)
    grad_down = jnp.stack([jnp.where(odd, other, same), jnp.where(odd, same, other)])

    expert_out = pl.pallas_call(
        out_kernel,
        out_shape=jax.ShapeDtypeStruct((slots_all, width), bf16),
        in_specs=[smem] + [vmem] * 2,
        out_specs=vmem,
        scratch_shapes=[
            pltpu.VMEM((CHIPS, 2, hid_rows, width), f32),
            pltpu.VMEM((up_cols, width), bf16),
        ],
        cost_estimate=pl.CostEstimate(
            flops=2 * slots_all * width * up_cols,
            bytes_accessed=7 << 20,
            transcendentals=0,
        ),
    )(info, weights, hidden)
    returned = exchange(expert_out.reshape(EXPERTS, CAP, width)).reshape(slots_all, width)
    logits = lax.dot_general(
        router_w, scaled, (((0,), (1,)), ((), ())), preferred_element_type=f32
    )
    gates = jnp.stack([logits[name] for name in NAMES])
    gates = jax.nn.sigmoid(gates)
    weight = pick.reshape(EXPERTS, CAP, tokens).astype(f32) * gates[:, None, :]
    weight = weight.reshape(slots_all, tokens)
    coarse = weight.astype(bf16)
    fine = (weight - coarse.astype(f32)).astype(bf16)
    dims = (((0,), (0,)), ((), ()))
    combined = lax.dot_general(
        coarse, returned, dims, preferred_element_type=f32
    ) + lax.dot_general(fine, returned, dims, preferred_element_type=f32)
    predicted = (residual + combined).astype(bf16)
    return (predicted, grad_down)


def solution(mesh):
    placed = (
        P(("dp", "expert"), None),
        P(("dp", "expert")),
        P(),
        P(),
        P(),
        P(),
        P(),
        P(),
        P("expert", "dp", None),
        P("expert", "dp", None),
        P(("dp", "expert"), None),
        P(("dp", "expert"), None),
    )
    return jax.shard_map(
        per_device,
        mesh=mesh,
        in_specs=placed,
        out_specs=(P(("dp", "expert"), None), P("expert", "dp", None)),
        check_vma=False,
    )
```

```python
import jax
import jax.numpy as jnp
from jax import lax
from jax.experimental import pallas as pl
from jax.experimental.pallas import tpu as pltpu
from jax.sharding import PartitionSpec as P

EXPERTS = 32
TOPK = 6
CAP = 32
PLANES = 16
CHIPS = 16
RING = 8
UP_ROWS = 32
PACK_ROWS = 48
STRIDE = 5
AXES = ("dp", "expert")


def home(z, k):
    return z ^ (10 * k)


NAMES = [2 * home(m // 2, m % 2) + m % 2 for m in range(EXPERTS)]


def cells():
    groups = []
    for core in range(2):
        for pair in range(RING):
            z = (2 * pair, 2 * pair + 1) if core == 0 else (2 * pair + 2, 2 * pair + 1)
            groups.append(
                [(2 * chip + core) * PLANES + z[odd] % PLANES for chip in range(CHIPS) for odd in range(2)]
            )
    return groups


def owners():
    return [
        [(2 * chip + core) * PLANES + z for z in range(k, PLANES, 2) for core in range(2)]
        for chip in range(CHIPS)
        for k in range(2)
    ]


def moves(flip, back):
    perm = []
    for chip in range(CHIPS):
        for core in range(2):
            for z in range(PLANES):
                k = core ^ flip
                place = (chip // 2 + STRIDE * z) % RING
                here = (2 * chip + core) * PLANES + z
                there = (2 * home(z, k) + chip % 2) * PLANES + 2 * place + k
                perm.append((there, here) if back else (here, there))
    return perm


def swap(pair, odd, back):
    same, other = jnp.where(odd, pair[1], pair[0]), jnp.where(odd, pair[0], pair[1])
    return (
        lax.ppermute(same, AXES, moves(0, back)),
        lax.ppermute(other, AXES, moves(1, back)),
    )


def across(rows):
    return lax.ppermute(rows, "dp", [(d, d ^ 1) for d in range(2 * CHIPS)])


def exchange(rows):
    return lax.all_to_all(
        rows, AXES, split_axis=0, concat_axis=0, tiled=True, axis_index_groups=cells()
    )


def dispatch_kernel(place_ref, tok_ref, cot_ref, out_ref):
    bf16 = jnp.bfloat16
    groups, tokens = place_ref.shape
    width = tok_ref.shape[1]
    step = 8
    slot = lax.broadcasted_iota(jnp.int32, (step, CAP, tokens), 1)
    for start in range(0, groups, step):
        place = place_ref[start : start + step, :]
        pick = (place[:, None, :] == slot).astype(jnp.float32).astype(bf16)
        pick = pick.reshape(step * CAP, tokens)
        for first, ref in ((0, tok_ref), (CAP, cot_ref)):
            rows = jnp.dot(pick, ref[...], preferred_element_type=jnp.float32).astype(bf16)
            out_ref[start : start + step, first : first + CAP, :] = rows.reshape(step, CAP, width)


def hidden_kernel(
    info, w_ref, got_ref, router_ref, hid_ref, keep_ref, give_ref, up_ref, gated_ref
):
    first, expert, core, k = info[0], info[1], info[2], info[3]
    f32, bf16 = jnp.float32, jnp.bfloat16
    cols = up_ref.shape[3]
    width = got_ref.shape[2]
    for chip in range(CHIPS):
        at = (first + chip // 2) & (RING - 1)
        for side in range(2):
            up_ref[chip, side] = w_ref[at, chip % 2, (k + side) & 1, :UP_ROWS, :cols]
    up = up_ref[...].reshape(width, cols)
    step = 8
    for start in range(0, EXPERTS, step):
        part = pl.ds(start * CAP, step * CAP)
        x = got_ref[start : start + step, :CAP, :].reshape(step * CAP, width)
        cot = got_ref[start : start + step, CAP:, :].reshape(step * CAP, width)
        pre = jnp.dot(x, up, preferred_element_type=f32)
        hid_ref[part, :] = jax.nn.gelu(pre, approximate=True).astype(bf16)
        gates = jax.nn.sigmoid(jnp.dot(x, router_ref[...], preferred_element_type=f32))
        mine = lax.broadcasted_iota(jnp.int32, gates.shape, 1) == expert
        gate = jnp.sum(jnp.where(mine, gates, 0.0), axis=1, keepdims=True)
        gated_ref[part, :] = (gate * cot.astype(f32)).astype(bf16)
    rows = keep_ref.shape[1]
    half = CHIPS // 2
    for j in range(2):
        grad = lax.dot_general(
            hid_ref[:, j * half * rows : (j + 1) * half * rows],
            gated_ref[...],
            (((0,), (0,)), ((), ())),
            preferred_element_type=f32,
        ).astype(bf16)

        def store(parity, ref, j=j, grad=grad):
            for i in range(parity, half, 2):
                at = (first + (j * half + i) // 2) & (RING - 1)
                ref[at] = grad[i * rows : (i + 1) * rows, :]

        @pl.when(core == 0)
        def _(store=store):
            store(0, keep_ref)
            store(1, give_ref)

        @pl.when(core == 1)
        def _(store=store):
            store(1, keep_ref)
            store(0, give_ref)


def out_kernel(info, w_ref, hid_ref, out_ref, wide_ref, down_ref):
    first, k = info[0], info[3]
    f32, bf16 = jnp.float32, jnp.bfloat16
    cols, width = hid_ref.shape[1], out_ref.shape[1]
    spare = width - cols
    full = PACK_ROWS - UP_ROWS
    tail = UP_ROWS * spare // width
    for chip in range(CHIPS):
        at = (first + chip // 2) & (RING - 1)
        for side in range(2):
            slot = (k + side) & 1
            wide_ref[chip, side, :full, :] = w_ref[at, chip % 2, slot, UP_ROWS:, :].astype(f32)
            rest = w_ref[at, chip % 2, slot, :UP_ROWS, cols:].astype(f32)
            for q in range(UP_ROWS // tail):
                wide_ref[chip, side, full:, q * spare : (q + 1) * spare] = rest[
                    q * tail : (q + 1) * tail, :
                ]
    down_ref[...] = wide_ref[...].reshape(cols, width).astype(bf16)
    rows = hid_ref.shape[0]
    step = 256
    for start in range(0, rows, step):
        part = pl.ds(start, step)
        out_ref[part, :] = jnp.dot(
            hid_ref[part, :], down_ref[...], preferred_element_type=f32
        ).astype(bf16)


def per_device(
    enc_out,
    actions,
    enc_gain,
    enc_bias,
    embed_w,
    action_table,
    pred_gain,
    router_w,
    up_w,
    down_w,
    cotangent,
    routes,
):
    bf16, f32 = jnp.bfloat16, jnp.float32
    tokens, width = cotangent.shape
    up_cols = up_w.shape[2]
    hid_rows = down_w.shape[1]
    device, z = lax.axis_index("dp"), lax.axis_index("expert")
    chip, core, k = device // 2, device % 2, z % 2
    odd = core == 1
    origin = chip ^ (10 * k)
    info = jnp.stack([STRIDE * origin % RING, 2 * origin + k, core, k]).astype(jnp.int32)

    spare = width - up_cols
    full = PACK_ROWS - UP_ROWS
    rest = down_w[:, full:, :].reshape(2, hid_rows - full, width // spare, spare)
    rest = rest.transpose(0, 2, 1, 3).reshape(2, UP_ROWS, spare)
    packed = jnp.concatenate(
        [jnp.concatenate([up_w, rest], axis=2), down_w[:, :full, :]], axis=1
    )
    own = swap(packed, odd, False)

    experts = jnp.array(NAMES, dtype=jnp.int32)
    hits = jnp.sum((routes.T[:, None, :] == experts[None, :, None]).astype(f32), axis=0)
    order = jnp.arange(tokens, dtype=jnp.int32)
    earlier = (order[:, None] < order[None, :]).astype(bf16)
    rank = jnp.dot(hits.astype(bf16), earlier, preferred_element_type=f32)
    place = jnp.where(hits > 0.0, rank.astype(jnp.int32), -1)
    slots = jnp.arange(CAP, dtype=jnp.int32)
    pick = (place[:, None, :] == slots[None, :, None]).reshape(EXPERTS * CAP, tokens)
    pick = pick.astype(bf16)

    encoded = enc_out.astype(f32)
    center = encoded - jnp.mean(encoded, axis=-1, keepdims=True)
    spread = jnp.mean(center * center, axis=-1, keepdims=True)
    normed = (center * lax.rsqrt(spread + 1e-06) * enc_gain + enc_bias).astype(bf16)
    onehot = (
        actions[:, None] == jnp.arange(action_table.shape[0], dtype=jnp.int32)[None, :]
    ).astype(bf16)
    residual = jnp.dot(normed, embed_w, preferred_element_type=f32) + jnp.dot(
        onehot, action_table, preferred_element_type=f32
    )
    scaled = (
        residual
        * lax.rsqrt(jnp.mean(residual * residual, axis=-1, keepdims=True) + 1e-06)
        * pred_gain
    ).astype(bf16)
    smem = pl.BlockSpec(memory_space=pltpu.SMEM)
    vmem = pl.BlockSpec(memory_space=pltpu.VMEM)
    sent = pl.pallas_call(
        dispatch_kernel,
        out_shape=jax.ShapeDtypeStruct((EXPERTS, 2 * CAP, width), bf16),
        in_specs=[vmem] * 3,
        out_specs=vmem,
        cost_estimate=pl.CostEstimate(
            flops=4 * EXPERTS * CAP * tokens * width, bytes_accessed=5 << 20, transcendentals=0
        ),
    )(place, scaled, cotangent)
    with jax.named_scope("tokens"):
        got = exchange(sent)
    own, sent = lax.optimization_barrier((own, sent))
    weights = lax.all_gather(
        jnp.stack(own), AXES, axis=0, tiled=True, axis_index_groups=owners()
    ).reshape(RING, 2, 2, PACK_ROWS, width)

    slots_all = EXPERTS * CAP
    hidden, keep, give = pl.pallas_call(
        hidden_kernel,
        out_shape=(
            jax.ShapeDtypeStruct((slots_all, up_cols), bf16),
            jax.ShapeDtypeStruct((RING, 2 * hid_rows, width), bf16),
            jax.ShapeDtypeStruct((RING, 2 * hid_rows, width), bf16),
        ),
        in_specs=[smem] + [vmem] * 3,
        out_specs=(vmem, vmem, vmem),
        scratch_shapes=[
            pltpu.VMEM((CHIPS, 2, UP_ROWS, up_cols), bf16),
            pltpu.VMEM((slots_all, width), bf16),
        ],
        cost_estimate=pl.CostEstimate(
            flops=4 * slots_all * width * up_cols,
            bytes_accessed=11 << 20,
            transcendentals=slots_all * up_cols,
        ),
    )(info, weights, got, router_w)
    pair = (keep.astype(f32) + across(give).astype(f32)).astype(bf16)
    parities = [list(range(k, PLANES, 2)) for k in range(2)]
    summed = lax.psum_scatter(
        pair, "expert", scatter_dimension=0, tiled=True, axis_index_groups=parities
    )
    same, other = swap(summed.reshape(2, hid_rows, width), k == 1, True)
    grad_down = jnp.stack([jnp.where(odd, other, same), jnp.where(odd, same, other)])

    expert_out = pl.pallas_call(
        out_kernel,
        out_shape=jax.ShapeDtypeStruct((slots_all, width), bf16),
        in_specs=[smem] + [vmem] * 2,
        out_specs=vmem,
        scratch_shapes=[
            pltpu.VMEM((CHIPS, 2, hid_rows, width), f32),
            pltpu.VMEM((up_cols, width), bf16),
        ],
        cost_estimate=pl.CostEstimate(
            flops=2 * slots_all * width * up_cols,
            bytes_accessed=7 << 20,
            transcendentals=0,
        ),
    )(info, weights, hidden)
    returned = exchange(expert_out.reshape(EXPERTS, CAP, width)).reshape(slots_all, width)
    logits = lax.dot_general(
        router_w, scaled, (((0,), (1,)), ((), ())), preferred_element_type=f32
    )
    gates = jnp.stack([logits[name] for name in NAMES])
    gates = jax.nn.sigmoid(gates)
    weight = pick.reshape(EXPERTS, CAP, tokens).astype(f32) * gates[:, None, :]
    weight = weight.reshape(slots_all, tokens)
    coarse = weight.astype(bf16)
    fine = (weight - coarse.astype(f32)).astype(bf16)
    dims = (((0,), (0,)), ((), ()))
    combined = lax.dot_general(
        coarse, returned, dims, preferred_element_type=f32
    ) + lax.dot_general(fine, returned, dims, preferred_element_type=f32)
    predicted = (residual + combined).astype(bf16)
    return (predicted, grad_down)


def solution(mesh):
    placed = (
        P(("dp", "expert"), None),
        P(("dp", "expert")),
        P(),
        P(),
        P(),
        P(),
        P(),
        P(),
        P("expert", "dp", None),
        P("expert", "dp", None),
        P(("dp", "expert"), None),
        P(("dp", "expert"), None),
    )
    return jax.shard_map(
        per_device,
        mesh=mesh,
        in_specs=placed,
        out_specs=(P(("dp", "expert"), None), P("expert", "dp", None)),
        check_vma=False,
    )
```

```python
import jax
import jax.numpy as jnp
from jax import lax
from jax.experimental import pallas as pl
from jax.experimental.pallas import tpu as pltpu
from jax.sharding import PartitionSpec as P

EXPERTS = 32
TOPK = 6
CAP = 32
PLANES = 16
CHIPS = 16
RING = 8
UP_ROWS = 32
PACK_ROWS = 48
STRIDE = 5
AXES = ("dp", "expert")


def home(z, k):
    return z ^ (10 * k)


NAMES = [2 * home(m // 2, m % 2) + m % 2 for m in range(EXPERTS)]


def cells():
    groups = []
    for core in range(2):
        for pair in range(RING):
            z = (2 * pair, 2 * pair + 1) if core == 0 else (2 * pair + 2, 2 * pair + 1)
            groups.append(
                [(2 * chip + core) * PLANES + z[odd] % PLANES for chip in range(CHIPS) for odd in range(2)]
            )
    return groups


def owners():
    return [
        [(2 * chip + core) * PLANES + z for z in range(k, PLANES, 2) for core in range(2)]
        for chip in range(CHIPS)
        for k in range(2)
    ]


def moves(flip, back):
    perm = []
    for chip in range(CHIPS):
        for core in range(2):
            for z in range(PLANES):
                k = core ^ flip
                place = (chip // 2 + STRIDE * z) % RING
                here = (2 * chip + core) * PLANES + z
                there = (2 * home(z, k) + chip % 2) * PLANES + 2 * place + k
                perm.append((there, here) if back else (here, there))
    return perm


def swap(pair, odd, back):
    same, other = jnp.where(odd, pair[1], pair[0]), jnp.where(odd, pair[0], pair[1])
    return (
        lax.ppermute(same, AXES, moves(0, back)),
        lax.ppermute(other, AXES, moves(1, back)),
    )


def across(rows):
    return lax.ppermute(rows, "dp", [(d, d ^ 1) for d in range(2 * CHIPS)])


def exchange(rows):
    return lax.all_to_all(
        rows, AXES, split_axis=0, concat_axis=0, tiled=True, axis_index_groups=cells()
    )


def dispatch_kernel(
    enc_ref, actions_ref, gain_ref, bias_ref, embed_ref, table_ref, scale_ref, routes_ref,
    names_ref, cot_ref, out_ref, residual_ref, scaled_ref, place_ref,
):
    f32, bf16 = jnp.float32, jnp.bfloat16
    encoded = enc_ref[...].astype(f32)
    center = encoded - jnp.mean(encoded, axis=-1, keepdims=True)
    spread = jnp.mean(center * center, axis=-1, keepdims=True)
    normed = (center * lax.rsqrt(spread + 1e-06) * gain_ref[...] + bias_ref[...]).astype(bf16)
    kinds = lax.broadcasted_iota(jnp.int32, (table_ref.shape[0], actions_ref.shape[1]), 0)
    onehot = (kinds == actions_ref[...]).astype(f32).astype(bf16)
    residual = jnp.dot(normed, embed_ref[...], preferred_element_type=f32) + lax.dot_general(
        onehot, table_ref[...], (((0,), (0,)), ((), ())), preferred_element_type=f32
    )
    residual_ref[...] = residual
    power = jnp.mean(residual * residual, axis=-1, keepdims=True)
    scaled = (residual * lax.rsqrt(power + 1e-06) * scale_ref[...]).astype(bf16)
    scaled_ref[...] = scaled

    groups, tokens = place_ref.shape
    width = scaled.shape[1]
    names = names_ref[...]
    hits = jnp.zeros((groups, tokens), f32)
    for k in range(routes_ref.shape[0]):
        hits = hits + (routes_ref[k : k + 1, :] == names).astype(f32)
    before = lax.broadcasted_iota(jnp.int32, (tokens, tokens), 0)
    after = lax.broadcasted_iota(jnp.int32, (tokens, tokens), 1)
    earlier = (before < after).astype(f32).astype(bf16)
    rank = jnp.dot(hits.astype(bf16), earlier, preferred_element_type=f32)
    places = jnp.where(hits > 0.0, rank.astype(jnp.int32), -1)
    place_ref[...] = places
    step = 8
    slot = lax.broadcasted_iota(jnp.int32, (step, CAP, tokens), 1)
    for start in range(0, groups, step):
        place = places[start : start + step, :]
        pick = (place[:, None, :] == slot).astype(f32).astype(bf16)
        pick = pick.reshape(step * CAP, tokens)
        for first, source in ((0, scaled), (CAP, cot_ref[...])):
            rows = jnp.dot(pick, source, preferred_element_type=f32).astype(bf16)
            out_ref[start : start + step, first : first + CAP, :] = rows.reshape(step, CAP, width)


def hidden_kernel(
    info, w_ref, got_ref, router_ref, hid_ref, keep_ref, give_ref, up_ref, gated_ref
):
    first, expert, core, k = info[0], info[1], info[2], info[3]
    f32, bf16 = jnp.float32, jnp.bfloat16
    cols = up_ref.shape[3]
    width = got_ref.shape[2]
    for chip in range(CHIPS):
        at = (first + chip // 2) & (RING - 1)
        for side in range(2):
            up_ref[chip, side] = w_ref[at, chip % 2, (k + side) & 1, :UP_ROWS, :cols]
    up = up_ref[...].reshape(width, cols)
    step = 8
    for start in range(0, EXPERTS, step):
        part = pl.ds(start * CAP, step * CAP)
        x = got_ref[start : start + step, :CAP, :].reshape(step * CAP, width)
        cot = got_ref[start : start + step, CAP:, :].reshape(step * CAP, width)
        pre = jnp.dot(x, up, preferred_element_type=f32)
        hid_ref[part, :] = jax.nn.gelu(pre, approximate=True).astype(bf16)
        gates = jax.nn.sigmoid(jnp.dot(x, router_ref[...], preferred_element_type=f32))
        mine = lax.broadcasted_iota(jnp.int32, gates.shape, 1) == expert
        gate = jnp.sum(jnp.where(mine, gates, 0.0), axis=1, keepdims=True)
        gated_ref[part, :] = (gate * cot.astype(f32)).astype(bf16)
    rows = keep_ref.shape[1]
    half = CHIPS // 2
    for j in range(2):
        grad = lax.dot_general(
            hid_ref[:, j * half * rows : (j + 1) * half * rows],
            gated_ref[...],
            (((0,), (0,)), ((), ())),
            preferred_element_type=f32,
        ).astype(bf16)

        def store(parity, ref, j=j, grad=grad):
            for i in range(parity, half, 2):
                at = (first + (j * half + i) // 2) & (RING - 1)
                ref[at] = grad[i * rows : (i + 1) * rows, :]

        @pl.when(core == 0)
        def _(store=store):
            store(0, keep_ref)
            store(1, give_ref)

        @pl.when(core == 1)
        def _(store=store):
            store(1, keep_ref)
            store(0, give_ref)


def out_kernel(info, w_ref, hid_ref, out_ref, wide_ref, down_ref):
    first, k = info[0], info[3]
    f32, bf16 = jnp.float32, jnp.bfloat16
    cols, width = hid_ref.shape[1], out_ref.shape[1]
    spare = width - cols
    full = PACK_ROWS - UP_ROWS
    tail = UP_ROWS * spare // width
    for chip in range(CHIPS):
        at = (first + chip // 2) & (RING - 1)
        for side in range(2):
            slot = (k + side) & 1
            wide_ref[chip, side, :full, :] = w_ref[at, chip % 2, slot, UP_ROWS:, :].astype(f32)
            rest = w_ref[at, chip % 2, slot, :UP_ROWS, cols:].astype(f32)
            for q in range(UP_ROWS // tail):
                wide_ref[chip, side, full:, q * spare : (q + 1) * spare] = rest[
                    q * tail : (q + 1) * tail, :
                ]
    down_ref[...] = wide_ref[...].reshape(cols, width).astype(bf16)
    rows = hid_ref.shape[0]
    step = 256
    for start in range(0, rows, step):
        part = pl.ds(start, step)
        out_ref[part, :] = jnp.dot(
            hid_ref[part, :], down_ref[...], preferred_element_type=f32
        ).astype(bf16)


def per_device(
    enc_out,
    actions,
    enc_gain,
    enc_bias,
    embed_w,
    action_table,
    pred_gain,
    router_w,
    up_w,
    down_w,
    cotangent,
    routes,
):
    bf16, f32 = jnp.bfloat16, jnp.float32
    tokens, width = cotangent.shape
    up_cols = up_w.shape[2]
    hid_rows = down_w.shape[1]
    device, z = lax.axis_index("dp"), lax.axis_index("expert")
    chip, core, k = device // 2, device % 2, z % 2
    odd = core == 1
    origin = chip ^ (10 * k)
    info = jnp.stack([STRIDE * origin % RING, 2 * origin + k, core, k]).astype(jnp.int32)

    spare = width - up_cols
    full = PACK_ROWS - UP_ROWS
    rest = down_w[:, full:, :].reshape(2, hid_rows - full, width // spare, spare)
    rest = rest.transpose(0, 2, 1, 3).reshape(2, UP_ROWS, spare)
    packed = jnp.concatenate(
        [jnp.concatenate([up_w, rest], axis=2), down_w[:, :full, :]], axis=1
    )
    own = swap(packed, odd, False)

    smem = pl.BlockSpec(memory_space=pltpu.SMEM)
    vmem = pl.BlockSpec(memory_space=pltpu.VMEM)
    sent, residual, scaled, place = pl.pallas_call(
        dispatch_kernel,
        out_shape=(
            jax.ShapeDtypeStruct((EXPERTS, 2 * CAP, width), bf16),
            jax.ShapeDtypeStruct((tokens, width), f32),
            jax.ShapeDtypeStruct((tokens, width), bf16),
            jax.ShapeDtypeStruct((EXPERTS, tokens), jnp.int32),
        ),
        in_specs=[vmem] * 10,
        out_specs=(vmem,) * 4,
        cost_estimate=pl.CostEstimate(
            flops=4 * EXPERTS * CAP * tokens * width, bytes_accessed=10 << 20, transcendentals=0
        ),
    )(
        enc_out,
        actions[None, :],
        enc_gain[None, :],
        enc_bias[None, :],
        embed_w,
        action_table,
        pred_gain[None, :],
        routes.T,
        jnp.array(NAMES, dtype=jnp.int32)[:, None],
        cotangent,
    )
    with jax.named_scope("tokens"):
        got = exchange(sent)
    own, sent = lax.optimization_barrier((own, sent))
    weights = lax.all_gather(
        jnp.stack(own), AXES, axis=0, tiled=True, axis_index_groups=owners()
    ).reshape(RING, 2, 2, PACK_ROWS, width)

    slots_all = EXPERTS * CAP
    hidden, keep, give = pl.pallas_call(
        hidden_kernel,
        out_shape=(
            jax.ShapeDtypeStruct((slots_all, up_cols), bf16),
            jax.ShapeDtypeStruct((RING, 2 * hid_rows, width), bf16),
            jax.ShapeDtypeStruct((RING, 2 * hid_rows, width), bf16),
        ),
        in_specs=[smem] + [vmem] * 3,
        out_specs=(vmem, vmem, vmem),
        scratch_shapes=[
            pltpu.VMEM((CHIPS, 2, UP_ROWS, up_cols), bf16),
            pltpu.VMEM((slots_all, width), bf16),
        ],
        cost_estimate=pl.CostEstimate(
            flops=4 * slots_all * width * up_cols,
            bytes_accessed=11 << 20,
            transcendentals=slots_all * up_cols,
        ),
    )(info, weights, got, router_w)
    pair = (keep.astype(f32) + across(give).astype(f32)).astype(bf16)
    parities = [list(range(k, PLANES, 2)) for k in range(2)]
    summed = lax.psum_scatter(
        pair, "expert", scatter_dimension=0, tiled=True, axis_index_groups=parities
    )
    same, other = swap(summed.reshape(2, hid_rows, width), k == 1, True)
    grad_down = jnp.stack([jnp.where(odd, other, same), jnp.where(odd, same, other)])

    expert_out = pl.pallas_call(
        out_kernel,
        out_shape=jax.ShapeDtypeStruct((slots_all, width), bf16),
        in_specs=[smem] + [vmem] * 2,
        out_specs=vmem,
        scratch_shapes=[
            pltpu.VMEM((CHIPS, 2, hid_rows, width), f32),
            pltpu.VMEM((up_cols, width), bf16),
        ],
        cost_estimate=pl.CostEstimate(
            flops=2 * slots_all * width * up_cols,
            bytes_accessed=7 << 20,
            transcendentals=0,
        ),
    )(info, weights, hidden)
    returned = exchange(expert_out.reshape(EXPERTS, CAP, width)).reshape(slots_all, width)
    logits = lax.dot_general(
        router_w, scaled, (((0,), (1,)), ((), ())), preferred_element_type=f32
    )
    gates = jnp.stack([logits[name] for name in NAMES])
    gates = jax.nn.sigmoid(gates)
    slots = jnp.arange(CAP, dtype=jnp.int32)
    pick = place[:, None, :] == slots[None, :, None]
    weight = jnp.where(pick, gates[:, None, :], 0.0)
    weight = weight.reshape(slots_all, tokens)
    coarse = weight.astype(bf16)
    fine = (weight - coarse.astype(f32)).astype(bf16)
    dims = (((0,), (0,)), ((), ()))
    combined = lax.dot_general(
        coarse, returned, dims, preferred_element_type=f32
    ) + lax.dot_general(fine, returned, dims, preferred_element_type=f32)
    predicted = (residual + combined).astype(bf16)
    return (predicted, grad_down)


def solution(mesh):
    placed = (
        P(("dp", "expert"), None),
        P(("dp", "expert")),
        P(),
        P(),
        P(),
        P(),
        P(),
        P(),
        P("expert", "dp", None),
        P("expert", "dp", None),
        P(("dp", "expert"), None),
        P(("dp", "expert"), None),
    )
    return jax.shard_map(
        per_device,
        mesh=mesh,
        in_specs=placed,
        out_specs=(P(("dp", "expert"), None), P("expert", "dp", None)),
        check_vma=False,
    )
```

```python
import jax
import jax.numpy as jnp
from jax import lax
from jax.experimental import pallas as pl
from jax.experimental.pallas import tpu as pltpu
from jax.sharding import PartitionSpec as P

EXPERTS = 32
TOPK = 6
CAP = 32
PLANES = 16
CHIPS = 16
RING = 8
UP_ROWS = 32
PACK_ROWS = 48
STRIDE = 5
AXES = ("dp", "expert")


def home(z, k):
    return z ^ (10 * k)


NAMES = [2 * home(m // 2, m % 2) + m % 2 for m in range(EXPERTS)]


def cells():
    groups = []
    for core in range(2):
        for pair in range(RING):
            z = (2 * pair, 2 * pair + 1) if core == 0 else (2 * pair + 2, 2 * pair + 1)
            groups.append(
                [(2 * chip + core) * PLANES + z[odd] % PLANES for chip in range(CHIPS) for odd in range(2)]
            )
    return groups


def owners():
    return [
        [(2 * chip + core) * PLANES + z for z in range(k, PLANES, 2) for core in range(2)]
        for chip in range(CHIPS)
        for k in range(2)
    ]


def moves(flip, back):
    perm = []
    for chip in range(CHIPS):
        for core in range(2):
            for z in range(PLANES):
                k = core ^ flip
                place = (chip // 2 + STRIDE * z) % RING
                here = (2 * chip + core) * PLANES + z
                there = (2 * home(z, k) + chip % 2) * PLANES + 2 * place + k
                perm.append((there, here) if back else (here, there))
    return perm


def swap(pair, odd, back):
    same, other = jnp.where(odd, pair[1], pair[0]), jnp.where(odd, pair[0], pair[1])
    return (
        lax.ppermute(same, AXES, moves(0, back)),
        lax.ppermute(other, AXES, moves(1, back)),
    )


def across(rows):
    return lax.ppermute(rows, "dp", [(d, d ^ 1) for d in range(2 * CHIPS)])


def exchange(rows):
    return lax.all_to_all(
        rows, AXES, split_axis=0, concat_axis=0, tiled=True, axis_index_groups=cells()
    )


def dispatch_kernel(
    enc_ref, actions_ref, gain_ref, bias_ref, embed_ref, table_ref, scale_ref, routes_ref,
    names_ref, cot_ref, out_ref, residual_ref, scaled_ref, place_ref,
):
    f32, bf16 = jnp.float32, jnp.bfloat16
    encoded = enc_ref[...].astype(f32)
    center = encoded - jnp.mean(encoded, axis=-1, keepdims=True)
    spread = jnp.mean(center * center, axis=-1, keepdims=True)
    normed = (center * lax.rsqrt(spread + 1e-06) * gain_ref[...] + bias_ref[...]).astype(bf16)
    kinds = lax.broadcasted_iota(jnp.int32, (table_ref.shape[0], actions_ref.shape[1]), 0)
    onehot = (kinds == actions_ref[...]).astype(f32).astype(bf16)
    residual = jnp.dot(normed, embed_ref[...], preferred_element_type=f32) + lax.dot_general(
        onehot, table_ref[...], (((0,), (0,)), ((), ())), preferred_element_type=f32
    )
    residual_ref[...] = residual
    power = jnp.mean(residual * residual, axis=-1, keepdims=True)
    scaled = (residual * lax.rsqrt(power + 1e-06) * scale_ref[...]).astype(bf16)
    scaled_ref[...] = scaled

    groups, tokens = place_ref.shape
    width = scaled.shape[1]
    names = names_ref[...]
    hits = jnp.zeros((groups, tokens), f32)
    for k in range(routes_ref.shape[0]):
        hits = hits + (routes_ref[k : k + 1, :] == names).astype(f32)
    before = lax.broadcasted_iota(jnp.int32, (tokens, tokens), 0)
    after = lax.broadcasted_iota(jnp.int32, (tokens, tokens), 1)
    earlier = (before < after).astype(f32).astype(bf16)
    rank = jnp.dot(hits.astype(bf16), earlier, preferred_element_type=f32)
    places = jnp.where(hits > 0.0, rank.astype(jnp.int32), -1)
    place_ref[...] = places
    step = 8
    slot = lax.broadcasted_iota(jnp.int32, (step, CAP, tokens), 1)
    for start in range(0, groups, step):
        place = places[start : start + step, :]
        pick = (place[:, None, :] == slot).astype(f32).astype(bf16)
        pick = pick.reshape(step * CAP, tokens)
        for first, source in ((0, scaled), (CAP, cot_ref[...])):
            rows = jnp.dot(pick, source, preferred_element_type=f32).astype(bf16)
            out_ref[start : start + step, first : first + CAP, :] = rows.reshape(step, CAP, width)


def hidden_kernel(
    info, w_ref, got_ref, router_ref, hid_ref, keep_ref, give_ref, up_ref, gated_ref, here_ref, sems
):
    first, expert, core, k = info[0], info[1], info[2], info[3]
    f32, bf16 = jnp.float32, jnp.bfloat16
    cols = up_ref.shape[3]
    width = got_ref.shape[2]
    step = 8
    loads = []
    for i in range(EXPERTS // step):
        part = pl.ds(i * step, step)
        loads.append(pltpu.make_async_copy(got_ref.at[part], here_ref.at[part], sems.at[i]))
        loads[i].start()
    for chip in range(CHIPS):
        at = (first + chip // 2) & (RING - 1)
        for side in range(2):
            up_ref[chip, side] = w_ref[at, chip % 2, (k + side) & 1, :UP_ROWS, :cols]
    up = up_ref[...].reshape(width, cols)
    for start in range(0, EXPERTS, step):
        loads[start // step].wait()
        part = pl.ds(start * CAP, step * CAP)
        x = here_ref[start : start + step, :CAP, :].reshape(step * CAP, width)
        cot = here_ref[start : start + step, CAP:, :].reshape(step * CAP, width)
        pre = jnp.dot(x, up, preferred_element_type=f32)
        hid_ref[part, :] = jax.nn.gelu(pre, approximate=True).astype(bf16)
        gates = jax.nn.sigmoid(jnp.dot(x, router_ref[...], preferred_element_type=f32))
        mine = lax.broadcasted_iota(jnp.int32, gates.shape, 1) == expert
        gate = jnp.sum(jnp.where(mine, gates, 0.0), axis=1, keepdims=True)
        gated_ref[part, :] = (gate * cot.astype(f32)).astype(bf16)
    rows = keep_ref.shape[1]
    half = CHIPS // 2
    for j in range(2):
        grad = lax.dot_general(
            hid_ref[:, j * half * rows : (j + 1) * half * rows],
            gated_ref[...],
            (((0,), (0,)), ((), ())),
            preferred_element_type=f32,
        ).astype(bf16)

        def store(parity, ref, j=j, grad=grad):
            for i in range(parity, half, 2):
                at = (first + (j * half + i) // 2) & (RING - 1)
                ref[at] = grad[i * rows : (i + 1) * rows, :]

        @pl.when(core == 0)
        def _(store=store):
            store(0, keep_ref)
            store(1, give_ref)

        @pl.when(core == 1)
        def _(store=store):
            store(1, keep_ref)
            store(0, give_ref)


def out_kernel(info, w_ref, hid_ref, out_ref, wide_ref, down_ref):
    first, k = info[0], info[3]
    f32, bf16 = jnp.float32, jnp.bfloat16
    cols, width = hid_ref.shape[1], out_ref.shape[1]
    spare = width - cols
    full = PACK_ROWS - UP_ROWS
    tail = UP_ROWS * spare // width
    for chip in range(CHIPS):
        at = (first + chip // 2) & (RING - 1)
        for side in range(2):
            slot = (k + side) & 1
            wide_ref[chip, side, :full, :] = w_ref[at, chip % 2, slot, UP_ROWS:, :].astype(f32)
            rest = w_ref[at, chip % 2, slot, :UP_ROWS, cols:].astype(f32)
            for q in range(UP_ROWS // tail):
                wide_ref[chip, side, full:, q * spare : (q + 1) * spare] = rest[
                    q * tail : (q + 1) * tail, :
                ]
    down_ref[...] = wide_ref[...].reshape(cols, width).astype(bf16)
    rows = hid_ref.shape[0]
    step = 256
    for start in range(0, rows, step):
        part = pl.ds(start, step)
        out_ref[part, :] = jnp.dot(
            hid_ref[part, :], down_ref[...], preferred_element_type=f32
        ).astype(bf16)


def per_device(
    enc_out,
    actions,
    enc_gain,
    enc_bias,
    embed_w,
    action_table,
    pred_gain,
    router_w,
    up_w,
    down_w,
    cotangent,
    routes,
):
    bf16, f32 = jnp.bfloat16, jnp.float32
    tokens, width = cotangent.shape
    up_cols = up_w.shape[2]
    hid_rows = down_w.shape[1]
    device, z = lax.axis_index("dp"), lax.axis_index("expert")
    chip, core, k = device // 2, device % 2, z % 2
    odd = core == 1
    origin = chip ^ (10 * k)
    info = jnp.stack([STRIDE * origin % RING, 2 * origin + k, core, k]).astype(jnp.int32)

    spare = width - up_cols
    full = PACK_ROWS - UP_ROWS
    rest = down_w[:, full:, :].reshape(2, hid_rows - full, width // spare, spare)
    rest = rest.transpose(0, 2, 1, 3).reshape(2, UP_ROWS, spare)
    packed = jnp.concatenate(
        [jnp.concatenate([up_w, rest], axis=2), down_w[:, :full, :]], axis=1
    )
    own = swap(packed, odd, False)

    smem = pl.BlockSpec(memory_space=pltpu.SMEM)
    vmem = pl.BlockSpec(memory_space=pltpu.VMEM)
    sent, residual, scaled, place = pl.pallas_call(
        dispatch_kernel,
        out_shape=(
            jax.ShapeDtypeStruct((EXPERTS, 2 * CAP, width), bf16),
            jax.ShapeDtypeStruct((tokens, width), f32),
            jax.ShapeDtypeStruct((tokens, width), bf16),
            jax.ShapeDtypeStruct((EXPERTS, tokens), jnp.int32),
        ),
        in_specs=[vmem] * 10,
        out_specs=(vmem,) * 4,
        cost_estimate=pl.CostEstimate(
            flops=4 * EXPERTS * CAP * tokens * width, bytes_accessed=10 << 20, transcendentals=0
        ),
    )(
        enc_out,
        actions[None, :],
        enc_gain[None, :],
        enc_bias[None, :],
        embed_w,
        action_table,
        pred_gain[None, :],
        routes.T,
        jnp.array(NAMES, dtype=jnp.int32)[:, None],
        cotangent,
    )
    with jax.named_scope("tokens"):
        got = exchange(sent)
    own, sent = lax.optimization_barrier((own, sent))
    weights = lax.all_gather(
        jnp.stack(own), AXES, axis=0, tiled=True, axis_index_groups=owners()
    ).reshape(RING, 2, 2, PACK_ROWS, width)

    slots_all = EXPERTS * CAP
    hidden, keep, give = pl.pallas_call(
        hidden_kernel,
        out_shape=(
            jax.ShapeDtypeStruct((slots_all, up_cols), bf16),
            jax.ShapeDtypeStruct((RING, 2 * hid_rows, width), bf16),
            jax.ShapeDtypeStruct((RING, 2 * hid_rows, width), bf16),
        ),
        in_specs=[smem, vmem, pl.BlockSpec(memory_space=pl.ANY), vmem],
        out_specs=(vmem, vmem, vmem),
        scratch_shapes=[
            pltpu.VMEM((CHIPS, 2, UP_ROWS, up_cols), bf16),
            pltpu.VMEM((slots_all, width), bf16),
            pltpu.VMEM((EXPERTS, 2 * CAP, width), bf16),
            pltpu.SemaphoreType.DMA((4,)),
        ],
        cost_estimate=pl.CostEstimate(
            flops=4 * slots_all * width * up_cols,
            bytes_accessed=11 << 20,
            transcendentals=slots_all * up_cols,
        ),
    )(info, weights, got, router_w)
    pair = (keep.astype(f32) + across(give).astype(f32)).astype(bf16)
    parities = [list(range(k, PLANES, 2)) for k in range(2)]
    summed = lax.psum_scatter(
        pair, "expert", scatter_dimension=0, tiled=True, axis_index_groups=parities
    )
    same, other = swap(summed.reshape(2, hid_rows, width), k == 1, True)
    grad_down = jnp.stack([jnp.where(odd, other, same), jnp.where(odd, same, other)])

    expert_out = pl.pallas_call(
        out_kernel,
        out_shape=jax.ShapeDtypeStruct((slots_all, width), bf16),
        in_specs=[smem] + [vmem] * 2,
        out_specs=vmem,
        scratch_shapes=[
            pltpu.VMEM((CHIPS, 2, hid_rows, width), f32),
            pltpu.VMEM((up_cols, width), bf16),
        ],
        cost_estimate=pl.CostEstimate(
            flops=2 * slots_all * width * up_cols,
            bytes_accessed=7 << 20,
            transcendentals=0,
        ),
    )(info, weights, hidden)
    returned = exchange(expert_out.reshape(EXPERTS, CAP, width)).reshape(slots_all, width)
    logits = lax.dot_general(
        router_w, scaled, (((0,), (1,)), ((), ())), preferred_element_type=f32
    )
    gates = jnp.stack([logits[name] for name in NAMES])
    gates = jax.nn.sigmoid(gates)
    slots = jnp.arange(CAP, dtype=jnp.int32)
    pick = place[:, None, :] == slots[None, :, None]
    weight = jnp.where(pick, gates[:, None, :], 0.0)
    weight = weight.reshape(slots_all, tokens)
    coarse = weight.astype(bf16)
    fine = (weight - coarse.astype(f32)).astype(bf16)
    dims = (((0,), (0,)), ((), ()))
    combined = lax.dot_general(
        coarse, returned, dims, preferred_element_type=f32
    ) + lax.dot_general(fine, returned, dims, preferred_element_type=f32)
    predicted = (residual + combined).astype(bf16)
    return (predicted, grad_down)


def solution(mesh):
    placed = (
        P(("dp", "expert"), None),
        P(("dp", "expert")),
        P(),
        P(),
        P(),
        P(),
        P(),
        P(),
        P("expert", "dp", None),
        P("expert", "dp", None),
        P(("dp", "expert"), None),
        P(("dp", "expert"), None),
    )
    return jax.shard_map(
        per_device,
        mesh=mesh,
        in_specs=placed,
        out_specs=(P(("dp", "expert"), None), P("expert", "dp", None)),
        check_vma=False,
    )
```
